256 devices in a mesh: blk: 128 (over y, z, x_lo, core), rhs: 2 (over x_hi).
Axes of the slice: x: 4 (x_hi: 2, x_lo: 2; x = x_hi * 2 + x_lo), y: 4, z: 8, core: 2. Of those that a mesh axis runs over, the one named last changes fastest.
Arguments:
- positions: float32 [3, 32768], P(None, 'blk'), may hold values from -1 to 1
- normal_angles: float32 [2, 32768], P(None, 'blk'), may hold values from -3.140625 to 3.140625
- areas: float32 [32768], P('blk'), may hold values from 1 to 6
- densities: float32 [2, 2, 32768], P('rhs', None, 'blk'), may hold values from -6 to 6
- need_owner: int32 [32768, 1], P('blk'), may hold values from 0 to 127; in each aligned block of 256 rows (0 to 255, 256 to 511, ...) at most 8 rows name the same one
- need_slot: int32 [32768], P('blk'), may hold values from 0 to 255
- near_index: int32 [32, 32768], P(None, 'blk'), may hold values from 0 to 255
- near_coef: float32 [2, 32, 32768], P(None, None, 'blk'), may hold values from -2 to 2
Outputs:
- result_field: float32 [2, 2, 32768], P('rhs', None, 'blk')
The draws below stay inside these ranges and needn't reach their ends.
Inputs may be any that keep to these rules, and one draw needn't show every extreme that they name: `need_owner`: among the 256 entries of one block of targets, at most 8 name the same owner.
All inputs are finite; a program needn't handle non-finite values.
Results may differ from the reference program's by a relative error of at most 0.0003.
Values sent between devices are 32-bit elements; how exact they have to be, the bound alone decides.
A program may use at most 128 MiB of HBM per device.

```python
import math
import jax
import jax.numpy as jnp
import numpy as np
from jax import lax

P_DEV = 256
NB = 32
NEED = 256
CAP = 8
PANELS = 32768
NEEDS = 32768
N_BLK = 128


def touch_ends(drawn, stream_key, least, high):
    spot = [jax.random.randint(jax.random.fold_in(stream_key, axis), (), 0, length) for axis, length in enumerate(drawn.shape)]
    widest = drawn.shape.index(max(drawn.shape))
    beside = spot[:widest] + [(spot[widest] + 1) % drawn.shape[widest]] + spot[widest + 1:]
    return drawn.at[tuple(spot)].set(least).at[tuple(beside)].set(high)


def block_scale(rng, dims, split, smallest, largest):
    gain = 1.0
    for position, shards_of in split:
        draws = jax.random.uniform(jax.random.fold_in(jax.random.fold_in(rng, 6), position), (shards_of,), jnp.float32, smallest / len(split), largest / len(split))
        gain = gain * jnp.repeat(jnp.exp(draws), dims[position] // shards_of).reshape((-1,) + (1,) * (len(dims) - 1 - position))
    return gain


def deal_out(stream_key, own, number, rows, amount, top, bound, slope):
    sequence = jax.random.permutation(stream_key, amount)
    crowded, usual = shares(amount, rows * top, bound, slope, True), shares(amount, rows * top, bound, slope, False)
    places = jnp.arange(amount)

    def named(tallies, offset_by):
        used = int((tallies > 0).sum())
        fixed = max(1, used // 4)
        shifted = fixed + (places - fixed + offset_by * (used - fixed)) % max(1, amount - fixed)
        return jnp.zeros((amount,), jnp.int32).at[sequence[jnp.where(places < fixed, places, shifted)]].set(jnp.asarray(tallies, jnp.int32))

    tallies = jnp.where(number % 4 == 0, named(crowded, number // 4), named(usual, number - number // 4 - 1))
    mixed = jax.random.permutation(jax.random.fold_in(own, 3), amount)
    giver, sink = mixed[0:amount // 2 * 2:2], mixed[1:amount // 2 * 2:2]
    slack = jnp.minimum(tallies[giver] - 1, bound - tallies[sink]) // 2
    slack = jnp.where((giver == sequence[0]) | (sink == sequence[0]) | (tallies[sink] == 0), 0, jnp.maximum(slack, 0))
    shifted = jax.random.randint(jax.random.fold_in(own, 4), (amount // 2,), 0, 1 << 20) % (slack + 1)
    tallies = tallies.at[giver].add(-shifted).at[sink].add(shifted)
    items = jnp.searchsorted(jnp.cumsum(tallies), jnp.arange(rows * top), side="right").astype(jnp.int32)
    table = items.reshape(top, rows).T
    table = table[jax.random.permutation(jax.random.fold_in(own, 1), rows)]
    offset_by = jax.random.randint(jax.random.fold_in(own, 2), (rows, 1), 0, top)
    return jnp.take_along_axis(table, (jnp.arange(top)[None, :] + offset_by) % top, axis=1)


def shares(count, total, bound, skew, full):
    loads = [(1 << 20) // math.isqrt(rank ** skew) + 1 for rank in range(1, count + 1)]
    largest = bound if full else min(bound, max(-(-total // count), total * loads[0] // sum(loads)))
    least = 1 if total - largest >= count - 1 else 0
    given, surplus = [largest] + [least] * (count - 1), total - largest - least * (count - 1)
    while surplus > 0:
        movable = [i for i in range(1, count) if given[i] < largest] or [i for i in range(1, count) if given[i] < bound]
        whole, budget = sum([loads[i] for i in movable]), surplus
        for i in movable:
            more = min(bound - given[i], max(1, budget * loads[i] // whole), surplus)
            given[i] = given[i] + more
            surplus = surplus - more
    return np.array(given)


def centred(rng, shape, width, bound, split=(), kind=jnp.bfloat16):
    array = jax.random.normal(rng, shape, jnp.float32) * width
    if len(split) > 0:
        array = block_scale(rng, shape, split, -0.22, 0.18) * array
    return jnp.clip(array, min=-bound, max=bound).astype(kind)


def setup_inputs(seed: int = 0) -> dict:
    splits = jax.random.split(jax.random.key(seed), 9)
    positions = jnp.clip(jax.random.uniform(splits[0], (3, PANELS), jnp.float32, -1.0, 1.0) * block_scale(splits[0], (3, PANELS), ((1, 128),), -0.4, 0.0), -1.0, 1.0)
    normal_angles = jnp.clip(jax.random.uniform(splits[1], (2, PANELS), jnp.float32, -3.140625, 3.140625), -3.140625, 3.140625)
    areas = jnp.clip(jnp.exp(math.log(6.0) - 1.7917595 * jax.random.uniform(splits[2], (PANELS,), jnp.float32) ** block_scale(splits[2], (PANELS,), ((0, 128),), -0.2, 0.2)), 1.0, 6.0)
    densities = centred(splits[3], (2, 2, PANELS), 1.0, 6.0, ((0, 2), (2, 128)), jnp.float32)
    need_owner_keys = jax.random.split(jax.random.fold_in(splits[4], 1), NEEDS // NEED)
    need_owner_turns = jax.random.permutation(jax.random.fold_in(splits[4], 3), NEEDS // NEED)
    need_owner = jax.vmap(lambda own, number: deal_out(jax.random.fold_in(splits[4], 2), own, number, NEED, N_BLK, 1, CAP, 2))(need_owner_keys, need_owner_turns).reshape((NEEDS, 1))
    need_slot = touch_ends(jax.random.randint(splits[5], (NEEDS,), 0, P_DEV), jax.random.fold_in(splits[5], 1), 0, P_DEV - 1).astype(jnp.int32)
    near_index = touch_ends(jax.random.randint(splits[6], (NB, PANELS), 0, NEED), jax.random.fold_in(splits[6], 1), 0, NEED - 1).astype(jnp.int32)
    near_coef = centred(splits[7], (2, NB, PANELS), 0.15, 2.0, ((2, 128),), jnp.float32)
    return {"positions": positions, "normal_angles": normal_angles, "areas": areas, "densities": densities, "need_owner": need_owner, "need_slot": need_slot, "near_index": near_index, "near_coef": near_coef}


WAVE = 8.0
COUPLE = 1.0
SOFT = 0.1

def unit_normals(angles):
    azimuth = angles[0]
    elevation = angles[1]
    return jnp.stack([jnp.cos(azimuth) * jnp.cos(elevation), jnp.sin(azimuth) * jnp.cos(elevation), jnp.sin(elevation)], 0)

def kernel_tile(targets, geometry):
    offset_vec = targets[:, :, None] - geometry[0:3, None, :]
    distance = jnp.sqrt(lax.optimization_barrier(jnp.sum(offset_vec * offset_vec, 0)) + SOFT * SOFT)
    facing = lax.optimization_barrier(jnp.sum(offset_vec * geometry[3:6, None, :], 0))
    single = 1.0 / (4.0 * math.pi * distance)
    double = facing * single / (distance * distance)
    phases = WAVE * distance
    cosine = jnp.cos(phases)
    sines = jnp.sin(phases)
    weight = geometry[6][None, :]
    real_part = weight * (double * (cosine + phases * sines) + COUPLE * single * sines)
    imag_part = weight * (double * (sines - phases * cosine) - COUPLE * single * cosine)
    return (real_part, imag_part)

def apply_tile(targets, geometry, sources):
    real_part, imag_part = kernel_tile(targets, geometry)
    highest = lax.Precision.HIGHEST
    src_real = sources[:, 0, :]
    src_imag = sources[:, 1, :]
    out_real = jnp.einsum('ts,rs->rt', real_part, src_real, precision=highest) - jnp.einsum('ts,rs->rt', imag_part, src_imag, precision=highest)
    out_imag = jnp.einsum('ts,rs->rt', real_part, src_imag, precision=highest) + jnp.einsum('ts,rs->rt', imag_part, src_real, precision=highest)
    return (out_real, out_imag)

def reference(positions, normal_angles, areas, densities, need_owner, need_slot, near_index, near_coef):
    normals = unit_normals(normal_angles)
    weights = areas * (1.0 / math.sqrt(PANELS))
    geometry = jnp.concatenate([positions, normals, weights[None, :]], 0)
    geo_blocks = geometry.reshape(7, N_BLK, P_DEV).transpose(1, 0, 2)
    src_blocks = densities.reshape(2, 2, N_BLK, P_DEV).transpose(2, 0, 1, 3)

    def accumulate(running, block_item):
        more_real, more_imag = apply_tile(positions, block_item[0], block_item[1])
        return ((running[0] + more_real, running[1] + more_imag), None)
    zeros_init = jnp.zeros((2, PANELS), jnp.float32)
    (far_real, far_imag), _ = lax.scan(accumulate, (zeros_init, zeros_init), (geo_blocks, src_blocks))
    need_ids = need_owner[:, 0].astype(jnp.int32) * P_DEV + need_slot.astype(jnp.int32)
    device_of = jnp.arange(PANELS, dtype=jnp.int32) // P_DEV
    need_rows = device_of[None, :] * NEED + near_index.astype(jnp.int32)
    picked = densities[:, :, need_ids[need_rows]]
    coef_real = near_coef[0]
    coef_imag = near_coef[1]
    near_real = lax.optimization_barrier(jnp.sum(coef_real * picked[:, 0] - coef_imag * picked[:, 1], 1))
    near_imag = lax.optimization_barrier(jnp.sum(coef_real * picked[:, 1] + coef_imag * picked[:, 0], 1))
    field_real = 0.5 * densities[:, 0] + far_real + near_real
    field_imag = 0.5 * densities[:, 1] + far_imag + near_imag
    return jnp.stack([field_real, field_imag], 1)
```

```python
import functools
import math

import jax
import jax.numpy as jnp
from jax import lax
from jax.experimental import pallas as pl
from jax.experimental.pallas import tpu as pltpu
from jax.sharding import PartitionSpec as P

F32 = jnp.float32
BF16 = jnp.bfloat16
MESH = pl.DeviceIdType.MESH

WAVE = 8.0
SOFT = 0.1
TWO_PI = 2.0 * math.pi
TURNS = WAVE / TWO_PI
TURNS2 = TURNS * TURNS
KAPPA = 1.0 / TWO_PI
MAGIC = 12582912.0

C0 = 2.221441438377396
C1 = -0.9135295479465378
C2 = 0.11267874257383814
C3 = -0.006494477491585805

NY, NZ, NX, NC = 4, 8, 2, 2
PAIRS = NY * NZ
CHUNK = 16


def half_circle(turns):
    v = turns - ((turns + MAGIC) - MAGIC)
    z = v * v
    s = v * (C0 + z * (C1 + z * (C2 + z * C3)))
    q = s * s
    w = 2.0 - q
    s2 = s * (w * lax.rsqrt(w))
    return 0.5 - s2 * s2, s2 * (1.0 - q)


def pair_kernel(turns2, facing):
    h = lax.rsqrt(turns2)
    cosine, sine = half_circle(turns2 * h)
    p = facing * (h * h)
    hk = h * KAPPA
    a = p * hk
    e = p + hk
    return a * cosine + e * sine, a * sine - e * cosine


def split3(x):
    hi = x.astype(BF16).astype(F32)
    rest = x - hi
    mid = rest.astype(BF16).astype(F32)
    return hi, mid, rest - mid


def split2(x):
    hi = x.astype(BF16)
    return hi, (x - hi.astype(F32)).astype(BF16)


def source_terms(geo):
    parts = split3(geo)
    count = geo.shape[1]
    row = lax.broadcasted_iota(jnp.int32, (4, count), 0)

    def stack(k):
        hi, mid, lo = (part[4 * k : 4 * k + 4] for part in parts)
        ones = jnp.where(row < 3, 1.0 if k == 0 else 0.0, 0.0)
        rows = [hi, mid, lo, hi, mid, hi, ones, jnp.zeros((4, count), F32)]
        return jnp.concatenate(rows, 0).astype(BF16)

    return jnp.concatenate([stack(0), stack(1)], 1)


def target_terms(pos):
    count = pos.shape[1]
    hi, mid, lo = split3(pos)
    square = split3(TURNS2 * jnp.sum(pos * pos, 0, keepdims=True))
    one = jnp.ones((1, count), F32)
    zero = jnp.zeros((1, count), F32)
    rows = [hi, one, hi, one, hi, one, mid, zero, mid, zero, lo, zero]
    rows += [square[0], square[1], square[2]] + [zero] * 5
    return jnp.concatenate(rows, 0).T.astype(BF16)


def alternating(i, n):
    odd = i % 2
    return odd * ((i + 1) // 2) + (1 - odd) * ((n - i // 2) % n)


def kernel(
    pos_ref, ang_ref, area_ref, den_ref, owner_ref, slot_ref, index_ref, coef_ref, out_ref,
    pkt, mine, other, tf, rf0, rf1, k0, k1, acc, part, got,
    swap_send, swap_recv, core_send, core_recv, x_send, x_recv, z_send, y_send, recv, end_send, end_recv,
):
    count = pos_ref.shape[1]
    blk = lax.axis_index("blk")
    rhs = lax.axis_index("rhs")
    core = blk % NC
    x = (blk // NC) % NX
    z = (blk // (NC * NX)) % NZ
    y = blk // (NC * NX * NZ)

    def at(yy, zz, xx, cc):
        return ((yy * NZ + zz) * NX + xx) * NC + cc

    core_peer = at(y, z, x, 1 - core)
    x_peer = at(y, z, 1 - x, core)

    barrier = pltpu.get_barrier_semaphore()
    pl.semaphore_signal(barrier, inc=1, device_id={"rhs": 1 - rhs}, device_id_type=MESH)
    for peer in (core_peer, x_peer):
        pl.semaphore_signal(barrier, inc=1, device_id={"blk": peer}, device_id_type=MESH)
    for step in range(1, NZ):
        peer = at(y, (z + step) % NZ, x, core)
        pl.semaphore_signal(barrier, inc=1, device_id={"blk": peer}, device_id_type=MESH)
    for step in range(1, NY):
        peer = at((y + step) % NY, z, x, core)
        pl.semaphore_signal(barrier, inc=1, device_id={"blk": peer}, device_id_type=MESH)

    pos = pos_ref[...]
    cosines, sines = half_circle(ang_ref[...] * KAPPA)
    cosines = 2.0 * cosines
    sines = 2.0 * sines
    normal = jnp.concatenate(
        [cosines[0:1] * cosines[1:2], sines[0:1] * cosines[1:2], sines[1:2]], 0
    )
    weight = area_ref[...] * (TURNS / math.sqrt(count * NY * NZ * NX * NC))
    density = den_ref[0]
    mine[...] = jnp.concatenate([density * weight, density], 0)
    geometry = jnp.concatenate(
        [
            (-2.0 * TURNS2) * pos,
            TURNS2 * (jnp.sum(pos * pos, 0, keepdims=True) + SOFT * SOFT),
            TURNS2 * normal,
            -TURNS2 * jnp.sum(pos * normal, 0, keepdims=True),
        ],
        0,
    )
    tf[...] = target_terms(pos)
    acc[...] = jnp.zeros_like(acc)
    k1[...] = jnp.zeros_like(k1)

    pl.semaphore_wait(barrier, 3 + (NZ - 1) + (NY - 1))

    is_owner = core == rhs

    def swap():
        return pltpu.make_async_remote_copy(
            src_ref=mine, dst_ref=other, send_sem=swap_send, recv_sem=swap_recv,
            device_id={"rhs": 1 - rhs}, device_id_type=MESH,
        )

    def core_copy():
        return pltpu.make_async_remote_copy(
            src_ref=pkt.at[0], dst_ref=pkt.at[0], send_sem=core_send, recv_sem=core_recv,
            device_id={"blk": core_peer}, device_id_type=MESH,
        )

    @pl.when(is_owner)
    def _():
        swap().wait_recv()
        a = mine[...]
        b = other[...]
        first = jnp.where(rhs == 0, a, b)
        second = jnp.where(rhs == 0, b, a)
        pkt[0, 0:8, :] = geometry
        pkt[0, 8:16, :] = jnp.concatenate(
            [first[0:1], second[0:1], first[1:2], second[1:2], first[2:3], second[2:3], first[3:4], second[3:4]], 0
        )
        core_copy().start()

    @pl.when(jnp.logical_not(is_owner))
    def _():
        swap().start()
        core_copy().wait_recv()

    x_copy = pltpu.make_async_remote_copy(
        src_ref=pkt.at[0], dst_ref=pkt.at[1], send_sem=x_send, recv_sem=x_recv,
        device_id={"blk": x_peer}, device_id_type=MESH,
    )
    x_copy.start()
    x_copy.wait_recv()

    def z_copy(i):
        peer = at(y, (z + NZ - alternating(i, NZ)) % NZ, x, core)
        return pltpu.make_async_remote_copy(
            src_ref=pkt.at[pl.ds(0, 2)], dst_ref=pkt.at[pl.ds(2 * i, 2)],
            send_sem=z_send.at[i], recv_sem=recv.at[i],
            device_id={"blk": peer}, device_id_type=MESH,
        )

    def y_copy(i, j):
        peer = at((y + NY - alternating(j, NY)) % NY, z, x, core)
        return pltpu.make_async_remote_copy(
            src_ref=pkt.at[pl.ds(2 * i, 2)], dst_ref=pkt.at[pl.ds(2 * (j * NZ + i), 2)],
            send_sem=y_send.at[j * NZ + i], recv_sem=recv.at[j * NZ + i],
            device_id={"blk": peer}, device_id_type=MESH,
        )

    for i in range(1, NZ):
        z_copy(i).start()
    for j in range(1, NY):
        y_copy(0, j).start()

    rf = (rf0, rf1)
    kk = (k0, k1)

    def products(p, b):
        rf[b][...] = jnp.dot(tf[...], source_terms(pkt[p, 0:8, :]), preferred_element_type=F32)

    def pairs(b):
        for c in range(count // CHUNK):
            rows = slice(c * CHUNK, (c + 1) * CHUNK)
            real, imag = pair_kernel(rf[b][rows, 0:count], rf[b][rows, count : 2 * count])
            real_hi, real_lo = split2(real)
            imag_hi, imag_lo = split2(imag)
            kk[b][rows, 0:count] = real_hi
            kk[b][rows, count : 2 * count] = real_lo
            kk[b][rows, 2 * count : 3 * count] = imag_hi
            kk[b][rows, 3 * count : 4 * count] = imag_lo

    def apply(p, b):
        terms = pkt[p, 8:12, :]
        turned = jnp.concatenate([-terms[2:4], terms[0:2]], 0)

        def both(v):
            hi = v.astype(BF16).astype(F32)
            return jnp.concatenate([hi, v - hi], 0).astype(BF16)

        real, imag = both(terms), both(turned)
        left = jnp.concatenate([real, real, imag, imag], 1)
        acc[...] += lax.dot_general(
            left, kk[b][...], (((1,), (1,)), ((), ())), preferred_element_type=F32
        )

    products(0, 0)

    def body(i, carry):
        p = 2 * i
        apply(jnp.maximum(p - 1, 0), 1)
        products(p + 1, 1)
        pairs(0)

        @pl.when(i + 1 < PAIRS)
        def _():
            pltpu.make_async_remote_copy(
                src_ref=pkt.at[pl.ds(0, 2)], dst_ref=pkt.at[pl.ds(2 * (i + 1), 2)],
                send_sem=x_send, recv_sem=recv.at[i + 1],
                device_id={"blk": x_peer}, device_id_type=MESH,
            ).wait_recv()

        @pl.when(i + 1 < NZ)
        def _():
            for j in range(1, NY):
                y_copy(i + 1, j).start()

        apply(p, 0)
        products(jnp.minimum(p + 2, 2 * PAIRS - 1), 0)
        pairs(1)
        return carry

    lax.fori_loop(0, PAIRS, body, 0)
    apply(2 * PAIRS - 1, 1)
    total = acc[...]
    far = total[0:4] + total[4:8]

    lanes = 128
    halves = count // lanes
    owner = owner_ref[...]
    slot = slot_ref[...]
    listed = [[jnp.zeros((8, lanes), F32) for _ in range(halves)] for _ in range(4)]
    sub = lax.broadcasted_iota(jnp.int32, (8, lanes), 0)
    for group in range(2 * PAIRS // 8):
        k = sub + 8 * group
        pair_i = k // 2
        dz = alternating(pair_i % NZ, NZ)
        dy = alternating(pair_i // NZ, NY)
        block = at((y + dy) % NY, (z + dz) % NZ, (x + k % 2) % NX, rhs)
        for h in range(halves):
            own = jnp.broadcast_to(owner[:, h * lanes : (h + 1) * lanes], (8, lanes))
            place = jnp.broadcast_to(slot[:, h * lanes : (h + 1) * lanes], (8, lanes))
            for t in range(halves):
                hit = jnp.logical_and(own == block, place // lanes == t)
                for c in range(4):
                    table = pkt[8 * group : 8 * group + 8, 12 + c, t * lanes : (t + 1) * lanes]
                    found = jnp.take_along_axis(table, place % lanes, axis=1)
                    listed[c][h] = listed[c][h] + jnp.where(hit, found, 0.0)
    listed = [[jnp.sum(v, 0, keepdims=True) for v in row] for row in listed]

    near = [[], [], [], []]
    neighbours = index_ref.shape[0]
    for h in range(halves):
        sums = [jnp.zeros((8, lanes), F32) for _ in range(4)]
        for m in range(neighbours // 8):
            rows = slice(8 * m, 8 * m + 8)
            cols = slice(h * lanes, (h + 1) * lanes)
            where_to = index_ref[rows, cols]
            looked = []
            for c in range(4):
                value = jnp.zeros((8, lanes), F32)
                for t in range(halves):
                    table = jnp.broadcast_to(listed[c][t], (8, lanes))
                    found = jnp.take_along_axis(table, where_to % lanes, axis=1)
                    value = jnp.where(where_to // lanes == t, found, value)
                looked.append(value)
            real, imag = coef_ref[0, rows, cols], coef_ref[1, rows, cols]
            for r in range(2):
                sums[r] = sums[r] + (real * looked[r] - imag * looked[2 + r])
                sums[2 + r] = sums[2 + r] + (real * looked[2 + r] + imag * looked[r])
        for c in range(4):
            near[c].append(jnp.sum(sums[c], 0, keepdims=True))
    near = jnp.concatenate([jnp.concatenate(row, 1) for row in near], 0)
    both_sides = far + near
    side0 = jnp.concatenate([both_sides[0:1], both_sides[2:3]], 0)
    side1 = jnp.concatenate([both_sides[1:2], both_sides[3:4]], 0)
    part[...] = jnp.where(rhs == 0, side1, side0)
    last = pltpu.make_async_remote_copy(
        src_ref=part, dst_ref=got, send_sem=end_send, recv_sem=end_recv,
        device_id={"rhs": 1 - rhs}, device_id_type=MESH,
    )
    last.start()

    @pl.when(is_owner)
    def _():
        core_copy().wait_send()

    @pl.when(jnp.logical_not(is_owner))
    def _():
        swap().wait_send()

    x_copy.wait_send()
    for i in range(1, NZ):
        z_copy(i).wait_send()

    def drain(i, carry):
        for j in range(1, NY):
            y_copy(i, j).wait_send()
        return carry

    lax.fori_loop(0, NZ, drain, 0)
    last.wait()
    out_ref[0] = 0.5 * density + jnp.where(rhs == 0, side0, side1) + got[...]


def on_device(
    positions, normal_angles, areas, densities, need_owner, need_slot, near_index, near_coef
):
    count = positions.shape[1]
    vmem = pl.BlockSpec(memory_space=pltpu.VMEM)
    dma = pltpu.SemaphoreType.DMA
    return pl.pallas_call(
        kernel,
        out_shape=jax.ShapeDtypeStruct((1, 2, count), F32),
        in_specs=[vmem] * 8,
        out_specs=vmem,
        scratch_shapes=[
            pltpu.VMEM((2 * PAIRS, 16, count), F32),
            pltpu.VMEM((4, count), F32),
            pltpu.VMEM((4, count), F32),
            pltpu.VMEM((count, 32), BF16),
            pltpu.VMEM((count, 2 * count), F32),
            pltpu.VMEM((count, 2 * count), F32),
            pltpu.VMEM((count, 4 * count), BF16),
            pltpu.VMEM((count, 4 * count), BF16),
            pltpu.VMEM((8, count), F32),
            pltpu.VMEM((2, count), F32),
            pltpu.VMEM((2, count), F32),
            dma, dma, dma, dma, dma, dma, dma((NZ,)), dma((PAIRS,)), dma((PAIRS,)), dma, dma,
        ],
        compiler_params=pltpu.CompilerParams(collective_id=0, has_side_effects=True),
        name="field",
    )(
        positions,
        normal_angles,
        areas.reshape(1, count),
        densities,
        need_owner.reshape(1, count),
        need_slot.reshape(1, count),
        near_index,
        near_coef,
    )


def solution(mesh):
    in_specs = (
        P(None, "blk"),
        P(None, "blk"),
        P("blk"),
        P("rhs", None, "blk"),
        P("blk", None),
        P("blk"),
        P(None, "blk"),
        P(None, None, "blk"),
    )
    return jax.shard_map(
        on_device, mesh=mesh, in_specs=in_specs, out_specs=P("rhs", None, "blk"), check_vma=False
    )
```

```python
import math

import jax
import jax.numpy as jnp
from jax import lax
from jax.experimental import pallas as pl
from jax.experimental.pallas import tpu as pltpu
from jax.sharding import PartitionSpec as P

F32 = jnp.float32
BF16 = jnp.bfloat16
MESH = pl.DeviceIdType.MESH

WAVE = 8.0
SOFT = 0.1
TWO_PI = 2.0 * math.pi
TURNS = WAVE / TWO_PI
TURNS2 = TURNS * TURNS
KAPPA = 1.0 / TWO_PI
MAGIC = 12582912.0

C0 = 2.221441438377396
C1 = -0.9135295479465378
C2 = 0.11267874257383814
C3 = -0.006494477491585805

NY, NZ, NQ = 4, 8, 4
SIDES = 2
SLOTS = NY * NZ // SIDES
CHUNK = 16
LIST_AT = 12
LANES = 128


def half_circle(turns):
    v = turns - ((turns + MAGIC) - MAGIC)
    z = v * v
    s = v * (C0 + z * (C1 + z * (C2 + z * C3)))
    q = s * s
    w = 2.0 - q
    s2 = s * (w * lax.rsqrt(w))
    return 0.5 - s2 * s2, s2 * (1.0 - q)


def pair_kernel(turns2, facing):
    h = lax.rsqrt(turns2)
    cosine, sine = half_circle(turns2 * h)
    p = facing * (h * h)
    hk = h * KAPPA
    a = p * hk
    e = p + hk
    return a * cosine + e * sine, a * sine - e * cosine


def split3(x):
    hi = x.astype(BF16).astype(F32)
    rest = x - hi
    mid = rest.astype(BF16).astype(F32)
    return hi, mid, rest - mid


def split2(x):
    hi = x.astype(BF16)
    return hi, (x - hi.astype(F32)).astype(BF16)


def source_terms(geo):
    parts = split3(geo)
    count = geo.shape[1]
    row = lax.broadcasted_iota(jnp.int32, (4, count), 0)

    def stack(k):
        hi, mid, lo = (part[4 * k : 4 * k + 4] for part in parts)
        ones = jnp.where(row < 3, 1.0 if k == 0 else 0.0, 0.0)
        rows = [hi, mid, lo, hi, mid, hi, ones, jnp.zeros((4, count), F32)]
        return jnp.concatenate(rows, 0).astype(BF16)

    return jnp.concatenate([stack(0), stack(1)], 1)


def target_terms(pos):
    count = pos.shape[1]
    hi, mid, lo = split3(pos)
    square = split3(TURNS2 * jnp.sum(pos * pos, 0, keepdims=True))
    one = jnp.ones((1, count), F32)
    zero = jnp.zeros((1, count), F32)
    rows = [hi, one, hi, one, hi, one, mid, zero, mid, zero, lo, zero]
    rows += [square[0], square[1], square[2]] + [zero] * 5
    return jnp.concatenate(rows, 0).T.astype(BF16)


def alternating(i, n):
    odd = i % 2
    return odd * ((i + 1) // 2) + (1 - odd) * ((n - i // 2) % n)


def z_offset(i, away):
    odd = i % 2
    return (1 - away) * 2 * alternating(i, NZ // 2) + away * ((1 - odd) * (i + 1) + odd * (NZ - i))


def kernel(
    pos_hbm, ang_hbm, area_hbm, den_hbm, owner_hbm, slot_hbm, index_hbm, coef_hbm, out_ref,
    pos_in, ang_in, area_in, den_in, owner_in, slot_in, index_in, coef_in,
    geo, den, mine, other, tpos, lists, tf, terms, left, rf0, rf1, k0, k1, acc,
    listed, listed_got, part, part_got,
    in_sem, swap_send, swap_recv, geo_send, geo_recv, den_send, den_recv,
    tpos_send, tpos_recv, lists_send, lists_recv, listed_send, listed_recv, part_send, part_recv,
):
    count = pos_hbm.shape[1]
    halves = count // LANES
    blk = lax.axis_index("blk")
    rhs = lax.axis_index("rhs")
    q = blk % NQ
    z = (blk // NQ) % NZ
    y = blk // (NQ * NZ)
    away = (z + rhs) % 2
    is_owner = away == 0

    def block(yy, zz, qq):
        return (yy * NZ + zz) * NQ + qq

    def device(b, r):
        return {"blk": b, "rhs": r}

    def column(n):
        other_q = (q + n // 2) % NQ
        other_r = (rhs + n % 2) % 2
        return other_q, other_r

    barrier = pltpu.get_barrier_semaphore()

    def greet_column(n, carry):
        cq, cr = column(n)
        pl.semaphore_signal(
            barrier, inc=1, device_id=device(block(y, z, cq), cr), device_id_type=MESH
        )
        return carry

    def greet_plane(n, carry):
        pl.semaphore_signal(
            barrier,
            inc=1,
            device_id=device(block((y + n // NZ) % NY, (z + n) % NZ, q), rhs),
            device_id_type=MESH,
        )
        return carry

    lax.fori_loop(1, 2 * NQ, greet_column, 0)
    lax.fori_loop(1, NY * NZ, greet_plane, 0)

    loads = [
        pltpu.make_async_copy(src, dst, in_sem.at[n])
        for n, (src, dst) in enumerate(
            [
                (pos_hbm, pos_in), (ang_hbm, ang_in), (area_hbm, area_in), (den_hbm, den_in),
                (owner_hbm, owner_in), (slot_hbm, slot_in), (index_hbm, index_in), (coef_hbm, coef_in),
            ]
        )
    ]
    for load in loads:
        load.start()
    for load in loads[:6]:
        load.wait()

    pos = pos_in[...]
    tpos[q] = pos
    lists[q] = jnp.concatenate([owner_in[...], slot_in[...]], 0)
    cosines, sines = half_circle(ang_in[...] * KAPPA)
    cosines = 2.0 * cosines
    sines = 2.0 * sines
    normal = jnp.concatenate(
        [cosines[0:1] * cosines[1:2], sines[0:1] * cosines[1:2], sines[1:2]], 0
    )
    weight = area_in[...] * (TURNS / math.sqrt(count * NY * NZ * NQ))
    density = den_in[0]
    mine[...] = jnp.concatenate([density * weight, density], 0)

    @pl.when(is_owner)
    def _():
        geo[0] = jnp.concatenate(
            [
                (-2.0 * TURNS2) * pos,
                TURNS2 * (jnp.sum(pos * pos, 0, keepdims=True) + SOFT * SOFT),
                TURNS2 * normal,
                -TURNS2 * jnp.sum(pos * normal, 0, keepdims=True),
            ],
            0,
        )

    acc[...] = jnp.zeros_like(acc)
    k1[...] = jnp.zeros_like(k1)
    left[...] = jnp.zeros_like(left)

    pl.semaphore_wait(barrier, 2 * NQ - 1 + NY * NZ - 1)

    swap = pltpu.make_async_remote_copy(
        src_ref=mine, dst_ref=other, send_sem=swap_send, recv_sem=swap_recv,
        device_id=device(blk, 1 - rhs), device_id_type=MESH,
    )

    def to_plane(n, src, dst, send, recv):
        slot, far_off = n // 2, n % 2
        zz = (z + NZ - z_offset(slot % NQ, far_off)) % NZ
        yy = (y + NY - alternating(slot // NQ, NY)) % NY
        return pltpu.make_async_remote_copy(
            src_ref=src.at[0], dst_ref=dst.at[slot], send_sem=send.at[n], recv_sem=recv.at[slot],
            device_id=device(block(yy, zz, q), rhs), device_id_type=MESH,
        )

    def geo_copy(n):
        return to_plane(n, geo, geo, geo_send, geo_recv)

    def den_copy(n):
        return to_plane(n, den, den, den_send, den_recv)

    def arrival(dst, recv, slot):
        return pltpu.make_async_remote_copy(
            src_ref=dst.at[0], dst_ref=dst.at[slot], send_sem=swap_send, recv_sem=recv.at[slot],
            device_id=device(blk, 1 - rhs), device_id_type=MESH,
        )

    def to_quarter(n, src, send, recv):
        return pltpu.make_async_remote_copy(
            src_ref=src.at[q], dst_ref=src.at[q], send_sem=send.at[n], recv_sem=recv.at[q],
            device_id=device(block(y, z, (q + n) % NQ), rhs), device_id_type=MESH,
        )

    def from_quarter(n, src, send, recv):
        theirs = (q + n) % NQ
        return pltpu.make_async_remote_copy(
            src_ref=src.at[q], dst_ref=src.at[theirs], send_sem=send.at[n], recv_sem=recv.at[theirs],
            device_id=device(block(y, z, theirs), rhs), device_id_type=MESH,
        )

    def to_column(n, src, dst, send, recv):
        cq, cr = column(n)
        return pltpu.make_async_remote_copy(
            src_ref=src.at[2 * cq + cr], dst_ref=dst.at[2 * q + rhs],
            send_sem=send.at[n], recv_sem=recv.at[2 * q + rhs],
            device_id=device(block(y, z, cq), cr), device_id_type=MESH,
        )

    def from_column(n, src, dst, send, recv):
        cq, cr = column(n)
        return pltpu.make_async_remote_copy(
            src_ref=src.at[2 * cq + cr], dst_ref=dst.at[2 * cq + cr],
            send_sem=send.at[n], recv_sem=recv.at[2 * cq + cr],
            device_id=device(block(y, z, cq), cr), device_id_type=MESH,
        )

    def each(first, last, act):
        def step(n, carry):
            act(n)
            return carry

        lax.fori_loop(first, last, step, 0)

    @pl.when(jnp.logical_not(is_owner))
    def _():
        swap.start()

    each(1, NQ, lambda n: to_quarter(n, tpos, tpos_send, tpos_recv).start())

    @pl.when(is_owner)
    def _():
        each(1, 2 * SLOTS, lambda n: geo_copy(n).start())

    each(1, NQ, lambda n: to_quarter(n, lists, lists_send, lists_recv).start())
    each(1, NQ, lambda n: from_quarter(n, tpos, tpos_send, tpos_recv).wait_recv())
    for j in range(NQ):
        tf[j] = target_terms(tpos[j])

    @pl.when(is_owner)
    def _():
        swap.wait_recv()
        a = mine[...]
        b = other[...]
        first = jnp.where(rhs == 0, a, b)
        second = jnp.where(rhs == 0, b, a)
        den[0] = jnp.concatenate(
            [first[0:1], second[0:1], first[1:2], second[1:2], first[2:3], second[2:3], first[3:4], second[3:4]], 0
        )
        each(1, 2 * SLOTS, lambda n: den_copy(n).start())

    @pl.when(jnp.logical_not(is_owner))
    def _():
        arrival(geo, geo_recv, 0).wait_recv()

    rf = (rf0, rf1)
    kk = (k0, k1)

    def products(j):
        rf[j % 2][...] = jnp.dot(tf[j], terms[...], preferred_element_type=F32)

    def pairs(j):
        b = j % 2
        for c in range(count // CHUNK):
            rows = slice(c * CHUNK, (c + 1) * CHUNK)
            real, imag = pair_kernel(rf[b][rows, 0:count], rf[b][rows, count : 2 * count])
            real_hi, real_lo = split2(real)
            imag_hi, imag_lo = split2(imag)
            kk[b][rows, 0:count] = real_hi
            kk[b][rows, count : 2 * count] = real_lo
            kk[b][rows, 2 * count : 3 * count] = imag_hi
            kk[b][rows, 3 * count : 4 * count] = imag_lo

    def apply(j):
        acc[j] += lax.dot_general(
            left[...], kk[j % 2][...], (((1,), (1,)), ((), ())), preferred_element_type=F32
        )

    def density_terms(p):
        rows = den[p, 0:4, :]
        turned = jnp.concatenate([-rows[2:4], rows[0:2]], 0)

        def both(v):
            hi = v.astype(BF16).astype(F32)
            return jnp.concatenate([hi, v - hi], 0).astype(BF16)

        real, imag = both(rows), both(turned)
        return jnp.concatenate([real, real, imag, imag], 1)

    terms[...] = source_terms(geo[0])
    products(0)

    def look_up():
        each(1, NQ, lambda n: from_quarter(n, lists, lists_send, lists_recv).wait_recv())
        sub = lax.broadcasted_iota(jnp.int32, (8, LANES), 0)
        for j in range(NQ):
            for h in range(halves):
                cols = slice(h * LANES, (h + 1) * LANES)
                own = jnp.broadcast_to(lists[j, 0:1, cols], (8, LANES))
                place = jnp.broadcast_to(lists[j, 1:2, cols], (8, LANES))
                found = [jnp.zeros((8, LANES), F32) for _ in range(4)]
                for group in range(SLOTS // 8):
                    k = sub + 8 * group
                    dz = z_offset(k % NQ, away)
                    dy = alternating(k // NQ, NY)
                    there = block((y + dy) % NY, (z + dz) % NZ, q)
                    for t in range(halves):
                        hit = jnp.logical_and(own == there, place // LANES == t)
                        for c in range(4):
                            table = den[8 * group : 8 * group + 8, 4 + c, t * LANES : (t + 1) * LANES]
                            value = jnp.take_along_axis(table, place % LANES, axis=1)
                            found[c] = found[c] + jnp.where(hit, value, 0.0)
                for c in range(4):
                    listed[2 * j + c % 2, c // 2 : c // 2 + 1, cols] = jnp.sum(found[c], 0, keepdims=True)
        each(1, 2 * NQ, lambda n: to_column(n, listed, listed_got, listed_send, listed_recv).start())

    def body(p, carry):
        @pl.when(jnp.logical_and(p <= LIST_AT, p + away > 0))
        def _():
            arrival(den, den_recv, p).wait_recv()

        @pl.when(p + 1 < SLOTS)
        def _():
            arrival(geo, geo_recv, p + 1).wait_recv()

        @pl.when(p == LIST_AT)
        def _():
            each(LIST_AT + 1, SLOTS, lambda s: arrival(den, den_recv, s).wait_recv())
            look_up()

        apply(3)
        products(1)
        pairs(0)
        left[...] = density_terms(p)
        apply(0)
        products(2)
        pairs(1)
        apply(1)
        products(3)
        pairs(2)
        terms[...] = source_terms(geo[jnp.minimum(p + 1, SLOTS - 1)])
        apply(2)
        products(0)
        pairs(3)
        return carry

    lax.fori_loop(0, SLOTS, body, 0)
    apply(3)
    for j in range(NQ):
        total = acc[j]
        far = total[0:4] + total[4:8]
        for r in range(2):
            part[2 * j + r] = jnp.concatenate([far[r : r + 1], far[2 + r : 3 + r]], 0)
    each(1, 2 * NQ, lambda n: to_column(n, part, part_got, part_send, part_recv).start())

    loads[6].wait()
    loads[7].wait()
    me = 2 * q + rhs
    listed_got[me] = listed[me]
    each(1, 2 * NQ, lambda n: from_column(n, listed, listed_got, listed_send, listed_recv).wait_recv())
    mine_listed = jnp.sum(listed_got[...], 0)
    near = [[], []]
    neighbours = index_hbm.shape[0]
    tables = [
        [
            jnp.broadcast_to(mine_listed[c : c + 1, t * LANES : (t + 1) * LANES], (8, LANES))
            for t in range(halves)
        ]
        for c in range(2)
    ]
    for h in range(halves):
        cols = slice(h * LANES, (h + 1) * LANES)
        sums = [jnp.zeros((8, LANES), F32) for _ in range(2)]
        for m in range(neighbours // 8):
            rows = slice(8 * m, 8 * m + 8)
            where_to = index_in[rows, cols]
            looked = []
            for c in range(2):
                value = jnp.zeros((8, LANES), F32)
                for t in range(halves):
                    found = jnp.take_along_axis(tables[c][t], where_to % LANES, axis=1)
                    value = jnp.where(where_to // LANES == t, found, value)
                looked.append(value)
            real, imag = coef_in[0, rows, cols], coef_in[1, rows, cols]
            sums[0] = sums[0] + (real * looked[0] - imag * looked[1])
            sums[1] = sums[1] + (real * looked[1] + imag * looked[0])
        for c in range(2):
            near[c].append(jnp.sum(sums[c], 0, keepdims=True))
    near = jnp.concatenate([jnp.concatenate(row, 1) for row in near], 0)

    part_got[me] = part[me]

    @pl.when(is_owner)
    def _():
        each(1, 2 * SLOTS, lambda n: geo_copy(n).wait_send())
        each(1, 2 * SLOTS, lambda n: den_copy(n).wait_send())

    @pl.when(jnp.logical_not(is_owner))
    def _():
        swap.wait_send()

    each(1, NQ, lambda n: to_quarter(n, tpos, tpos_send, tpos_recv).wait_send())
    each(1, NQ, lambda n: to_quarter(n, lists, lists_send, lists_recv).wait_send())
    each(1, 2 * NQ, lambda n: to_column(n, listed, listed_got, listed_send, listed_recv).wait_send())
    each(1, 2 * NQ, lambda n: to_column(n, part, part_got, part_send, part_recv).wait_send())
    each(1, 2 * NQ, lambda n: from_column(n, part, part_got, part_send, part_recv).wait_recv())
    out_ref[0] = 0.5 * density + near + jnp.sum(part_got[...], 0)


def on_device(
    positions, normal_angles, areas, densities, need_owner, need_slot, near_index, near_coef
):
    count = positions.shape[1]
    args = (
        positions,
        normal_angles,
        areas.reshape(1, count),
        densities,
        need_owner.reshape(1, count),
        need_slot.reshape(1, count),
        near_index,
        near_coef,
    )
    dma = pltpu.SemaphoreType.DMA
    return pl.pallas_call(
        kernel,
        out_shape=jax.ShapeDtypeStruct((1, 2, count), F32),
        in_specs=[pl.BlockSpec(memory_space=pl.ANY)] * 8,
        out_specs=pl.BlockSpec(memory_space=pltpu.VMEM),
        scratch_shapes=[pltpu.VMEM(arg.shape, arg.dtype) for arg in args]
        + [
            pltpu.VMEM((SLOTS, 8, count), F32),
            pltpu.VMEM((SLOTS, 8, count), F32),
            pltpu.VMEM((4, count), F32),
            pltpu.VMEM((4, count), F32),
            pltpu.VMEM((NQ, 3, count), F32),
            pltpu.VMEM((NQ, 2, count), jnp.int32),
            pltpu.VMEM((NQ, count, 32), BF16),
            pltpu.VMEM((32, 2 * count), BF16),
            pltpu.VMEM((8, 4 * count), BF16),
            pltpu.VMEM((count, 2 * count), F32),
            pltpu.VMEM((count, 2 * count), F32),
            pltpu.VMEM((count, 4 * count), BF16),
            pltpu.VMEM((count, 4 * count), BF16),
            pltpu.VMEM((NQ, 8, count), F32),
            pltpu.VMEM((2 * NQ, 2, count), F32),
            pltpu.VMEM((2 * NQ, 2, count), F32),
            pltpu.VMEM((2 * NQ, 2, count), F32),
            pltpu.VMEM((2 * NQ, 2, count), F32),
            dma((8,)), dma, dma,
            dma((2 * SLOTS,)), dma((SLOTS,)), dma((2 * SLOTS,)), dma((SLOTS,)),
            dma((NQ,)), dma((NQ,)), dma((NQ,)), dma((NQ,)),
            dma((2 * NQ,)), dma((2 * NQ,)), dma((2 * NQ,)), dma((2 * NQ,)),
        ],
        compiler_params=pltpu.CompilerParams(collective_id=0, has_side_effects=True),
        name="field",
    )(*args)


def solution(mesh):
    in_specs = (
        P(None, "blk"),
        P(None, "blk"),
        P("blk"),
        P("rhs", None, "blk"),
        P("blk", None),
        P("blk"),
        P(None, "blk"),
        P(None, None, "blk"),
    )
    return jax.shard_map(
        on_device, mesh=mesh, in_specs=in_specs, out_specs=P("rhs", None, "blk"), check_vma=False
    )
```

```python
import math

import jax
import jax.numpy as jnp
from jax import lax
from jax.experimental import pallas as pl
from jax.experimental.pallas import tpu as pltpu
from jax.sharding import PartitionSpec as P

F32 = jnp.float32
BF16 = jnp.bfloat16
MESH = pl.DeviceIdType.MESH

WAVE = 8.0
SOFT = 0.1
TWO_PI = 2.0 * math.pi
TURNS = WAVE / TWO_PI
TURNS2 = TURNS * TURNS
KAPPA = 1.0 / TWO_PI

C0 = 2.221441438377396
C1 = -0.9135295479465378
C2 = 0.11267874257383814
C3 = -0.006494477491585805

NY, NZ, NQ = 4, 8, 4
SIDES = 2
SLOTS = NY * NZ // SIDES
CHUNK = 16
LIST_AT = 12
LANES = 128


def half_circle(turns):
    v = turns - jnp.round(turns)
    z = v * v
    s = v * (C0 + z * (C1 + z * (C2 + z * C3)))
    q = s * s
    w = 2.0 - q
    s2 = s * (w * lax.rsqrt(w))
    return 0.5 - s2 * s2, s2 * (1.0 - q)


def pair_kernel(turns2, facing):
    h = lax.rsqrt(turns2)
    cosine, sine = half_circle(turns2 * h)
    p = facing * (h * h)
    hk = h * KAPPA
    a = p * hk
    e = p + hk
    return a * cosine + e * sine, a * sine - e * cosine


def split3(x):
    hi = x.astype(BF16).astype(F32)
    rest = x - hi
    mid = rest.astype(BF16).astype(F32)
    return hi, mid, rest - mid


def split2(x):
    hi = x.astype(BF16)
    return hi, (x - hi.astype(F32)).astype(BF16)


def source_terms(geo):
    parts = split3(geo)
    count = geo.shape[1]
    row = lax.broadcasted_iota(jnp.int32, (4, count), 0)

    def stack(k):
        hi, mid, lo = (part[4 * k : 4 * k + 4] for part in parts)
        ones = jnp.where(row < 3, 1.0 if k == 0 else 0.0, 0.0)
        rows = [hi, mid, lo, hi, mid, hi, ones, jnp.zeros((4, count), F32)]
        return jnp.concatenate(rows, 0).T.astype(BF16)

    return jnp.concatenate([stack(0), stack(1)], 0)


def target_terms(pos):
    count = pos.shape[1]
    hi, mid, lo = split3(pos)
    square = split3(TURNS2 * jnp.sum(pos * pos, 0, keepdims=True))
    one = jnp.ones((1, count), F32)
    zero = jnp.zeros((1, count), F32)
    rows = [hi, one, hi, one, hi, one, mid, zero, mid, zero, lo, zero]
    rows += [square[0], square[1], square[2]] + [zero] * 5
    return jnp.concatenate(rows, 0).astype(BF16)


def alternating(i, n):
    odd = i % 2
    return odd * ((i + 1) // 2) + (1 - odd) * ((n - i // 2) % n)


def z_offset(i, away):
    odd = i % 2
    return (1 - away) * 2 * alternating(i, NZ // 2) + away * ((1 - odd) * (i + 1) + odd * (NZ - i))


def kernel(
    pos_hbm, ang_hbm, area_hbm, den_hbm, owner_hbm, slot_hbm, index_hbm, coef_hbm, out_ref,
    pos_in, ang_in, area_in, den_in, owner_in, slot_in, index_in, coef_in,
    geo, den, mine, other, tpos, lists, tf, terms, left, rf0, rf1, k0, k1, k2, k3, k4, k5, k6, k7, acc,
    listed, listed_got, part, part_got,
    in_sem, swap_send, swap_recv, geo_send, geo_recv, den_send, den_recv,
    tpos_send, tpos_recv, lists_send, lists_recv, listed_send, listed_recv, part_send, part_recv,
):
    count = pos_hbm.shape[1]
    halves = count // LANES
    blk = lax.axis_index("blk")
    rhs = lax.axis_index("rhs")
    q = blk % NQ
    z = (blk // NQ) % NZ
    y = blk // (NQ * NZ)
    away = (z + rhs) % 2
    is_owner = away == 0

    def block(yy, zz, qq):
        return (yy * NZ + zz) * NQ + qq

    def device(b, r):
        return {"blk": b, "rhs": r}

    def column(n):
        other_q = (q + n // 2) % NQ
        other_r = (rhs + n % 2) % 2
        return other_q, other_r

    barrier = pltpu.get_barrier_semaphore()

    def greet_column(n, carry):
        cq, cr = column(n)
        pl.semaphore_signal(
            barrier, inc=1, device_id=device(block(y, z, cq), cr), device_id_type=MESH
        )
        return carry

    def greet_plane(n, carry):
        pl.semaphore_signal(
            barrier,
            inc=1,
            device_id=device(block((y + n // NZ) % NY, (z + n) % NZ, q), rhs),
            device_id_type=MESH,
        )
        return carry

    lax.fori_loop(1, 2 * NQ, greet_column, 0)
    lax.fori_loop(1, NY * NZ, greet_plane, 0)

    loads = [
        pltpu.make_async_copy(src, dst, in_sem.at[n])
        for n, (src, dst) in enumerate(
            [
                (pos_hbm, pos_in), (ang_hbm, ang_in), (area_hbm, area_in), (den_hbm, den_in),
                (owner_hbm, owner_in), (slot_hbm, slot_in), (index_hbm, index_in), (coef_hbm, coef_in),
            ]
        )
    ]
    for load in loads:
        load.start()
    for load in loads[:6]:
        load.wait()

    pos = pos_in[...]
    tpos[q] = pos
    lists[q] = jnp.concatenate([owner_in[...], slot_in[...]], 0)
    cosines, sines = half_circle(ang_in[...] * KAPPA)
    cosines = 2.0 * cosines
    sines = 2.0 * sines
    normal = jnp.concatenate(
        [cosines[0:1] * cosines[1:2], sines[0:1] * cosines[1:2], sines[1:2]], 0
    )
    weight = area_in[...] * (TURNS / math.sqrt(count * NY * NZ * NQ))
    density = den_in[0]
    mine[...] = jnp.concatenate([density * weight, density], 0)

    @pl.when(is_owner)
    def _():
        geo[0] = jnp.concatenate(
            [
                (-2.0 * TURNS2) * pos,
                TURNS2 * (jnp.sum(pos * pos, 0, keepdims=True) + SOFT * SOFT),
                TURNS2 * normal,
                -TURNS2 * jnp.sum(pos * normal, 0, keepdims=True),
            ],
            0,
        )

    acc[...] = jnp.zeros_like(acc)
    for buffer in (k4, k5, k6, k7):
        buffer[...] = jnp.zeros_like(buffer)
    left[...] = jnp.zeros_like(left)

    pl.semaphore_wait(barrier, 2 * NQ - 1 + NY * NZ - 1)

    swap = pltpu.make_async_remote_copy(
        src_ref=mine, dst_ref=other, send_sem=swap_send, recv_sem=swap_recv,
        device_id=device(blk, 1 - rhs), device_id_type=MESH,
    )

    def to_plane(n, src, dst, send, recv):
        slot, far_off = n // 2, n % 2
        zz = (z + NZ - z_offset(slot % NQ, far_off)) % NZ
        yy = (y + NY - alternating(slot // NQ, NY)) % NY
        return pltpu.make_async_remote_copy(
            src_ref=src.at[0], dst_ref=dst.at[slot], send_sem=send.at[n], recv_sem=recv.at[slot],
            device_id=device(block(yy, zz, q), rhs), device_id_type=MESH,
        )

    def geo_copy(n):
        return to_plane(n, geo, geo, geo_send, geo_recv)

    def den_copy(n):
        return to_plane(n, den, den, den_send, den_recv)

    def arrival(dst, recv, slot):
        return pltpu.make_async_remote_copy(
            src_ref=dst.at[0], dst_ref=dst.at[slot], send_sem=swap_send, recv_sem=recv.at[slot],
            device_id=device(blk, 1 - rhs), device_id_type=MESH,
        )

    def to_quarter(n, src, send, recv):
        return pltpu.make_async_remote_copy(
            src_ref=src.at[q], dst_ref=src.at[q], send_sem=send.at[n], recv_sem=recv.at[q],
            device_id=device(block(y, z, (q + n) % NQ), rhs), device_id_type=MESH,
        )

    def from_quarter(n, src, send, recv):
        theirs = (q + n) % NQ
        return pltpu.make_async_remote_copy(
            src_ref=src.at[q], dst_ref=src.at[theirs], send_sem=send.at[n], recv_sem=recv.at[theirs],
            device_id=device(block(y, z, theirs), rhs), device_id_type=MESH,
        )

    def to_column(n, src, dst, send, recv):
        cq, cr = column(n)
        return pltpu.make_async_remote_copy(
            src_ref=src.at[2 * cq + cr], dst_ref=dst.at[2 * q + rhs],
            send_sem=send.at[n], recv_sem=recv.at[2 * q + rhs],
            device_id=device(block(y, z, cq), cr), device_id_type=MESH,
        )

    def from_column(n, src, dst, send, recv):
        cq, cr = column(n)
        return pltpu.make_async_remote_copy(
            src_ref=src.at[2 * cq + cr], dst_ref=dst.at[2 * cq + cr],
            send_sem=send.at[n], recv_sem=recv.at[2 * cq + cr],
            device_id=device(block(y, z, cq), cr), device_id_type=MESH,
        )

    def each(first, last, act):
        def step(n, carry):
            act(n)
            return carry

        lax.fori_loop(first, last, step, 0)

    @pl.when(jnp.logical_not(is_owner))
    def _():
        swap.start()

    each(1, NQ, lambda n: to_quarter(n, tpos, tpos_send, tpos_recv).start())

    @pl.when(is_owner)
    def _():
        each(1, 2 * SLOTS, lambda n: geo_copy(n).start())

    each(1, NQ, lambda n: to_quarter(n, lists, lists_send, lists_recv).start())
    each(1, NQ, lambda n: from_quarter(n, tpos, tpos_send, tpos_recv).wait_recv())
    for j in range(NQ):
        tf[j] = target_terms(tpos[j])

    @pl.when(is_owner)
    def _():
        swap.wait_recv()
        a = mine[...]
        b = other[...]
        first = jnp.where(rhs == 0, a, b)
        second = jnp.where(rhs == 0, b, a)
        den[0] = jnp.concatenate(
            [first[0:1], second[0:1], first[1:2], second[1:2], first[2:3], second[2:3], first[3:4], second[3:4]], 0
        )
        each(1, 2 * SLOTS, lambda n: den_copy(n).start())

    @pl.when(jnp.logical_not(is_owner))
    def _():
        arrival(geo, geo_recv, 0).wait_recv()

    rf = (rf0, rf1)
    kk = (k0, k1, k2, k3, k4, k5, k6, k7)

    def products(j):
        for half in range(2):
            rows = slice(half * count, (half + 1) * count)
            rf[j % 2][rows] = jnp.dot(terms[rows], tf[j % NQ], preferred_element_type=F32)

    def pairs(j, b):
        for c in range(count // CHUNK):
            rows = slice(c * CHUNK, (c + 1) * CHUNK)
            real, imag = pair_kernel(
                rf[j % 2][rows], rf[j % 2][count + c * CHUNK : count + (c + 1) * CHUNK]
            )
            for n, piece in enumerate(split2(real) + split2(imag)):
                kk[b][n * count + c * CHUNK : n * count + (c + 1) * CHUNK] = piece

    def apply(j, b):
        acc[j] += jnp.dot(left[...], kk[b][...], preferred_element_type=F32)

    def density_terms(p):
        rows = den[p, 0:4, :]
        turned = jnp.concatenate([-rows[2:4], rows[0:2]], 0)

        def both(v):
            hi = v.astype(BF16).astype(F32)
            return jnp.concatenate([hi, v - hi], 0).astype(BF16)

        real, imag = both(rows), both(turned)
        return jnp.concatenate([real, real, imag, imag], 1)

    terms[...] = source_terms(geo[0])
    products(0)

    def look_up():
        each(1, NQ, lambda n: from_quarter(n, lists, lists_send, lists_recv).wait_recv())
        sub = lax.broadcasted_iota(jnp.int32, (8, LANES), 0)
        for j in range(NQ):
            for h in range(halves):
                cols = slice(h * LANES, (h + 1) * LANES)
                own = jnp.broadcast_to(lists[j, 0:1, cols], (8, LANES))
                place = jnp.broadcast_to(lists[j, 1:2, cols], (8, LANES))
                found = [jnp.zeros((8, LANES), F32) for _ in range(4)]
                for group in range(SLOTS // 8):
                    k = sub + 8 * group
                    dz = z_offset(k % NQ, away)
                    dy = alternating(k // NQ, NY)
                    there = block((y + dy) % NY, (z + dz) % NZ, q)
                    for t in range(halves):
                        hit = jnp.logical_and(own == there, place // LANES == t)
                        for c in range(4):
                            table = den[8 * group : 8 * group + 8, 4 + c, t * LANES : (t + 1) * LANES]
                            value = jnp.take_along_axis(table, place % LANES, axis=1)
                            found[c] = found[c] + jnp.where(hit, value, 0.0)
                for c in range(4):
                    listed[2 * j + c % 2, c // 2 : c // 2 + 1, cols] = jnp.sum(found[c], 0, keepdims=True)
        each(1, 2 * NQ, lambda n: to_column(n, listed, listed_got, listed_send, listed_recv).start())

    def packet(p, now):
        then = 1 - now

        @pl.when(jnp.logical_and(p <= LIST_AT, p + away > 1))
        def _():
            arrival(den, den_recv, p - 1).wait_recv()

        @pl.when(p + 1 < SLOTS)
        def _():
            arrival(geo, geo_recv, p + 1).wait_recv()

        if now == LIST_AT % 2:

            @pl.when(p == LIST_AT)
            def _():
                each(LIST_AT, SLOTS, lambda s: arrival(den, den_recv, s).wait_recv())
                look_up()

        @pl.when(p > 0)
        def _():
            left[...] = density_terms(p - 1)

        for j in range(NQ):
            apply(j, NQ * then + j)
            if j == NQ - 1:
                terms[...] = source_terms(geo[jnp.minimum(p + 1, SLOTS - 1)])
            products(j + 1)
            pairs(j, NQ * now + j)

    def body(i, carry):
        packet(2 * i, 0)
        packet(2 * i + 1, 1)
        return carry

    lax.fori_loop(0, SLOTS // 2, body, 0)
    left[...] = density_terms(SLOTS - 1)
    for j in range(NQ):
        apply(j, NQ + j)
    for j in range(NQ):
        total = acc[j]
        far = total[0:4] + total[4:8]
        for r in range(2):
            part[2 * j + r] = jnp.concatenate([far[r : r + 1], far[2 + r : 3 + r]], 0)
    each(1, 2 * NQ, lambda n: to_column(n, part, part_got, part_send, part_recv).start())

    loads[6].wait()
    loads[7].wait()
    me = 2 * q + rhs
    listed_got[me] = listed[me]
    each(1, 2 * NQ, lambda n: from_column(n, listed, listed_got, listed_send, listed_recv).wait_recv())
    mine_listed = jnp.sum(listed_got[...], 0)
    near = [[], []]
    neighbours = index_hbm.shape[0]
    tables = [
        [
            jnp.broadcast_to(mine_listed[c : c + 1, t * LANES : (t + 1) * LANES], (8, LANES))
            for t in range(halves)
        ]
        for c in range(2)
    ]
    for h in range(halves):
        cols = slice(h * LANES, (h + 1) * LANES)
        sums = [jnp.zeros((8, LANES), F32) for _ in range(2)]
        for m in range(neighbours // 8):
            rows = slice(8 * m, 8 * m + 8)
            where_to = index_in[rows, cols]
            looked = []
            for c in range(2):
                value = jnp.zeros((8, LANES), F32)
                for t in range(halves):
                    found = jnp.take_along_axis(tables[c][t], where_to % LANES, axis=1)
                    value = jnp.where(where_to // LANES == t, found, value)
                looked.append(value)
            real, imag = coef_in[0, rows, cols], coef_in[1, rows, cols]
            sums[0] = sums[0] + (real * looked[0] - imag * looked[1])
            sums[1] = sums[1] + (real * looked[1] + imag * looked[0])
        for c in range(2):
            near[c].append(jnp.sum(sums[c], 0, keepdims=True))
    near = jnp.concatenate([jnp.concatenate(row, 1) for row in near], 0)

    part_got[me] = part[me]

    @pl.when(is_owner)
    def _():
        each(1, 2 * SLOTS, lambda n: geo_copy(n).wait_send())
        each(1, 2 * SLOTS, lambda n: den_copy(n).wait_send())

    @pl.when(jnp.logical_not(is_owner))
    def _():
        swap.wait_send()

    each(1, NQ, lambda n: to_quarter(n, tpos, tpos_send, tpos_recv).wait_send())
    each(1, NQ, lambda n: to_quarter(n, lists, lists_send, lists_recv).wait_send())
    each(1, 2 * NQ, lambda n: to_column(n, listed, listed_got, listed_send, listed_recv).wait_send())
    each(1, 2 * NQ, lambda n: to_column(n, part, part_got, part_send, part_recv).wait_send())
    each(1, 2 * NQ, lambda n: from_column(n, part, part_got, part_send, part_recv).wait_recv())
    out_ref[0] = 0.5 * density + near + jnp.sum(part_got[...], 0)


def on_device(
    positions, normal_angles, areas, densities, need_owner, need_slot, near_index, near_coef
):
    count = positions.shape[1]
    args = (
        positions,
        normal_angles,
        areas.reshape(1, count),
        densities,
        need_owner.reshape(1, count),
        need_slot.reshape(1, count),
        near_index,
        near_coef,
    )
    dma = pltpu.SemaphoreType.DMA
    return pl.pallas_call(
        kernel,
        out_shape=jax.ShapeDtypeStruct((1, 2, count), F32),
        in_specs=[pl.BlockSpec(memory_space=pl.ANY)] * 8,
        out_specs=pl.BlockSpec(memory_space=pltpu.VMEM),
        scratch_shapes=[pltpu.VMEM(arg.shape, arg.dtype) for arg in args]
        + [
            pltpu.VMEM((SLOTS, 8, count), F32),
            pltpu.VMEM((SLOTS, 8, count), F32),
            pltpu.VMEM((4, count), F32),
            pltpu.VMEM((4, count), F32),
            pltpu.VMEM((NQ, 3, count), F32),
            pltpu.VMEM((NQ, 2, count), jnp.int32),
            pltpu.VMEM((NQ, 32, count), BF16),
            pltpu.VMEM((2 * count, 32), BF16),
            pltpu.VMEM((8, 4 * count), BF16),
            pltpu.VMEM((2 * count, count), F32),
            pltpu.VMEM((2 * count, count), F32),
        ]
        + [pltpu.VMEM((4 * count, count), BF16)] * (2 * NQ)
        + [
            pltpu.VMEM((NQ, 8, count), F32),
            pltpu.VMEM((2 * NQ, 2, count), F32),
            pltpu.VMEM((2 * NQ, 2, count), F32),
            pltpu.VMEM((2 * NQ, 2, count), F32),
            pltpu.VMEM((2 * NQ, 2, count), F32),
            dma((8,)), dma, dma,
            dma((2 * SLOTS,)), dma((SLOTS,)), dma((2 * SLOTS,)), dma((SLOTS,)),
            dma((NQ,)), dma((NQ,)), dma((NQ,)), dma((NQ,)),
            dma((2 * NQ,)), dma((2 * NQ,)), dma((2 * NQ,)), dma((2 * NQ,)),
        ],
        compiler_params=pltpu.CompilerParams(collective_id=0, has_side_effects=True),
        name="field",
    )(*args)


def solution(mesh):
    in_specs = (
        P(None, "blk"),
        P(None, "blk"),
        P("blk"),
        P("rhs", None, "blk"),
        P("blk", None),
        P("blk"),
        P(None, "blk"),
        P(None, None, "blk"),
    )
    return jax.shard_map(
        on_device, mesh=mesh, in_specs=in_specs, out_specs=P("rhs", None, "blk"), check_vma=False
    )
```

```python
import math

import jax
import jax.numpy as jnp
from jax import lax
from jax.experimental import pallas as pl
from jax.experimental.pallas import tpu as pltpu
from jax.sharding import PartitionSpec as P

F32 = jnp.float32
BF16 = jnp.bfloat16
MESH = pl.DeviceIdType.MESH

WAVE = 8.0
SOFT = 0.1
TWO_PI = 2.0 * math.pi
TURNS = WAVE / TWO_PI
TURNS2 = TURNS * TURNS
KAPPA = 1.0 / TWO_PI

C0 = 2.221441438377396
C1 = -0.9135295479465378
C2 = 0.11267874257383814
C3 = -0.006494477491585805

NY, NZ, NQ = 4, 8, 4
BLOCKS = NY * NZ
PACKETS = BLOCKS // 2
EARLY = 8
CHUNK = 16
LIST_AT = 12
LANES = 128


def ring(d, n):
    return min(d, n - d)


OFFSETS = sorted(
    ((dy, dz) for dy in range(NY) for dz in range(NZ)),
    key=lambda o: (ring(o[0], NY) + ring(o[1], NZ), o),
)


def half_circle(turns):
    v = turns - jnp.round(turns)
    z = v * v
    s = v * (C0 + z * (C1 + z * (C2 + z * C3)))
    q = s * s
    w = 2.0 - q
    s2 = s * (w * lax.rsqrt(w))
    return 0.5 - s2 * s2, s2 * (1.0 - q)


def pair_kernel(turns2, facing):
    h = lax.rsqrt(turns2)
    cosine, sine = half_circle(turns2 * h)
    p = facing * (h * h)
    hk = h * KAPPA
    a = p * hk
    e = p + hk
    return a * cosine + e * sine, a * sine - e * cosine


def split3(x):
    hi = x.astype(BF16).astype(F32)
    rest = x - hi
    mid = rest.astype(BF16).astype(F32)
    return hi, mid, rest - mid


def split2(x):
    hi = x.astype(BF16)
    return hi, (x - hi.astype(F32)).astype(BF16)


def source_terms(geo):
    parts = split3(geo)
    count = geo.shape[1]
    row = lax.broadcasted_iota(jnp.int32, (4, count), 0)

    def stack(k):
        hi, mid, lo = (part[4 * k : 4 * k + 4] for part in parts)
        ones = jnp.where(row < 3, 1.0 if k == 0 else 0.0, 0.0)
        rows = [hi, mid, lo, hi, mid, hi, ones, jnp.zeros((4, count), F32)]
        return jnp.concatenate(rows, 0).T.astype(BF16)

    return jnp.concatenate([stack(0), stack(1)], 0)


def target_terms(pos):
    count = pos.shape[1]
    hi, mid, lo = split3(pos)
    square = split3(TURNS2 * jnp.sum(pos * pos, 0, keepdims=True))
    one = jnp.ones((1, count), F32)
    zero = jnp.zeros((1, count), F32)
    rows = [hi, one, hi, one, hi, one, mid, zero, mid, zero, lo, zero]
    rows += [square[0], square[1], square[2]] + [zero] * 5
    return jnp.concatenate(rows, 0).astype(BF16)


def kernel(
    pos_hbm, ang_hbm, area_hbm, den_hbm, owner_hbm, slot_hbm, index_hbm, coef_hbm, out_ref,
    pos_in, ang_in, area_in, den_in, owner_in, slot_in, index_in, coef_in,
    pkt, mine, other, tpos, lists, tf, terms, left, rf0, rf1, k0, k1, k2, k3, k4, k5, k6, k7, acc,
    listed, listed_got, part, part_got,
    in_sem, swap_send, swap_recv, pkt_send, pkt_recv, den_send, den_recv,
    tpos_send, tpos_recv, lists_send, lists_recv, listed_send, listed_recv, part_send, part_recv,
):
    count = pos_hbm.shape[1]
    halves = count // LANES
    blk = lax.axis_index("blk")
    rhs = lax.axis_index("rhs")
    q = blk % NQ
    z = (blk // NQ) % NZ
    y = blk // (NQ * NZ)
    column_base = blk - q
    side = 1 - rhs
    zs = [lax.rem(z + d, NZ) * NQ + q for d in range(NZ)]
    ys = [lax.rem(y + d, NY) * (NZ * NQ) for d in range(NY)]
    qs = [lax.rem(q + d, NQ) for d in range(NQ)]

    def device(b, r):
        return {"blk": b, "rhs": r}

    def column(n):
        return qs[n // 2], (side if n % 2 else rhs)

    def plane(n):
        dy, dz = OFFSETS[n]
        return device(ys[(NY - dy) % NY] + zs[(NZ - dz) % NZ], rhs)

    barrier = pltpu.get_barrier_semaphore()
    for n in range(BLOCKS - 1, 0, -1):
        pl.semaphore_signal(barrier, inc=1, device_id=plane(n), device_id_type=MESH)
    for n in range(1, 2 * NQ):
        cq, cr = column(n)
        pl.semaphore_signal(
            barrier, inc=1, device_id=device(column_base + cq, cr), device_id_type=MESH
        )

    loads = [
        pltpu.make_async_copy(src, dst, in_sem.at[n])
        for n, (src, dst) in enumerate(
            [
                (pos_hbm, pos_in), (ang_hbm, ang_in), (area_hbm, area_in), (den_hbm, den_in),
                (owner_hbm, owner_in), (slot_hbm, slot_in), (index_hbm, index_in), (coef_hbm, coef_in),
            ]
        )
    ]
    for load in loads:
        load.start()
    for load in loads[:6]:
        load.wait()

    def own_half(v):
        return jnp.where(rhs == 0, v[:, 0:LANES], v[:, LANES : 2 * LANES])

    def other_half(v):
        return jnp.where(rhs == 0, v[:, LANES : 2 * LANES], v[:, 0:LANES])

    pos = pos_in[...]
    tpos[q] = pos
    lists[q] = jnp.concatenate([owner_in[...], slot_in[...]], 0)
    cosines, sines = half_circle(ang_in[...] * KAPPA)
    cosines = 2.0 * cosines
    sines = 2.0 * sines
    normal = jnp.concatenate(
        [cosines[0:1] * cosines[1:2], sines[0:1] * cosines[1:2], sines[1:2]], 0
    )
    weight = area_in[...] * (TURNS / math.sqrt(count * BLOCKS * NQ))
    density = den_in[0]
    sources = jnp.concatenate([density * weight, density], 0)
    mine[...] = other_half(sources)
    pkt[0, 0:8, 0:LANES] = own_half(
        jnp.concatenate(
            [
                (-2.0 * TURNS2) * pos,
                TURNS2 * (jnp.sum(pos * pos, 0, keepdims=True) + SOFT * SOFT),
                TURNS2 * normal,
                -TURNS2 * jnp.sum(pos * normal, 0, keepdims=True),
            ],
            0,
        )
    )

    pl.semaphore_wait(barrier, 2 * NQ - 1 + BLOCKS - 1)

    swap = pltpu.make_async_remote_copy(
        src_ref=mine, dst_ref=other, send_sem=swap_send, recv_sem=swap_recv,
        device_id=device(blk, side), device_id_type=MESH,
    )

    def lanes_of(n):
        return pl.ds((n % 2) * LANES, LANES)

    def plane_copy(n, rows, send, recv):
        return pltpu.make_async_remote_copy(
            src_ref=pkt.at[0, rows, pl.ds(0, LANES)], dst_ref=pkt.at[n // 2, rows, lanes_of(n)],
            send_sem=send.at[n], recv_sem=recv.at[n],
            device_id=plane(n), device_id_type=MESH,
        )

    geo_rows, den_rows, all_rows = pl.ds(0, 8), pl.ds(8, 8), pl.ds(0, 16)

    def arrival(k, half, rows, recv):
        return pltpu.make_async_remote_copy(
            src_ref=pkt.at[0, rows, pl.ds(0, LANES)],
            dst_ref=pkt.at[k, rows, pl.ds(half * LANES, LANES)],
            send_sem=swap_send, recv_sem=recv.at[2 * k + half],
            device_id=device(blk, side), device_id_type=MESH,
        )

    def sent(n, rows, send):
        return pltpu.make_async_remote_copy(
            src_ref=pkt.at[0, rows, pl.ds(0, LANES)], dst_ref=pkt.at[0, rows, pl.ds(0, LANES)],
            send_sem=send.at[n], recv_sem=swap_recv,
            device_id=device(blk, side), device_id_type=MESH,
        )

    def to_quarter(n, src, send, recv):
        return pltpu.make_async_remote_copy(
            src_ref=src.at[q], dst_ref=src.at[q], send_sem=send.at[n], recv_sem=recv.at[q],
            device_id=device(column_base + qs[n], rhs), device_id_type=MESH,
        )

    def from_quarter(n, src, send, recv):
        return pltpu.make_async_remote_copy(
            src_ref=src.at[q], dst_ref=src.at[qs[n]], send_sem=send.at[n], recv_sem=recv.at[qs[n]],
            device_id=device(column_base + qs[n], rhs), device_id_type=MESH,
        )

    def to_column(n, src, dst, send, recv):
        cq, cr = column(n)
        return pltpu.make_async_remote_copy(
            src_ref=src.at[2 * cq + cr], dst_ref=dst.at[2 * q + rhs],
            send_sem=send.at[n], recv_sem=recv.at[2 * q + rhs],
            device_id=device(column_base + cq, cr), device_id_type=MESH,
        )

    def from_column(n, src, dst, send, recv):
        cq, cr = column(n)
        return pltpu.make_async_remote_copy(
            src_ref=src.at[2 * cq + cr], dst_ref=dst.at[2 * cq + cr],
            send_sem=send.at[n], recv_sem=recv.at[2 * cq + cr],
            device_id=device(column_base + cq, cr), device_id_type=MESH,
        )

    def each(first, last, act):
        for n in range(first, last):
            act(n)

    def loop(first, last, act):
        def step(n, carry):
            act(n)
            return carry

        lax.fori_loop(first, last, step, 0)

    swap.start()
    each(1, NQ, lambda n: to_quarter(n, tpos, tpos_send, tpos_recv).start())
    each(1, EARLY, lambda n: plane_copy(n, geo_rows, pkt_send, pkt_recv).start())
    each(1, NQ, lambda n: to_quarter(n, lists, lists_send, lists_recv).start())

    def send_densities():
        swap.wait_recv()
        a = own_half(sources)
        b = other[...]
        first = jnp.where(rhs == 0, a, b)
        second = jnp.where(rhs == 0, b, a)
        pkt[0, 8:16, 0:LANES] = jnp.concatenate(
            [first[0:1], second[0:1], first[1:2], second[1:2], first[2:3], second[2:3], first[3:4], second[3:4]], 0
        )
        each(1, EARLY, lambda n: plane_copy(n, den_rows, den_send, den_recv).start())
        each(EARLY, BLOCKS, lambda n: plane_copy(n, all_rows, pkt_send, pkt_recv).start())

    each(1, NQ, lambda n: from_quarter(n, tpos, tpos_send, tpos_recv).wait_recv())
    for j in range(NQ):
        tf[j] = target_terms(tpos[j])
    arrival(0, 1, geo_rows, pkt_recv).wait_recv()

    rf = (rf0, rf1)
    kk = (k0, k1, k2, k3, k4, k5, k6, k7)

    def products(j):
        for half in range(2):
            rows = slice(half * count, (half + 1) * count)
            rf[j % 2][rows] = jnp.dot(terms[rows], tf[j % NQ], preferred_element_type=F32)

    def pairs(j, b):
        for c in range(count // CHUNK):
            rows = slice(c * CHUNK, (c + 1) * CHUNK)
            real, imag = pair_kernel(
                rf[j % 2][rows], rf[j % 2][count + c * CHUNK : count + (c + 1) * CHUNK]
            )
            for n, piece in enumerate(split2(real) + split2(imag)):
                kk[b][n * count + c * CHUNK : n * count + (c + 1) * CHUNK] = piece

    def apply(j, b):
        acc[j] += jnp.dot(left[...], kk[b][...], preferred_element_type=F32)

    def density_terms(p):
        rows = pkt[p, 8:12, :]
        turned = jnp.concatenate([-rows[2:4], rows[0:2]], 0)

        def both(v):
            hi = v.astype(BF16).astype(F32)
            return jnp.concatenate([hi, v - hi], 0).astype(BF16)

        real, imag = both(rows), both(turned)
        return jnp.concatenate([real, real, imag, imag], 1)

    terms[...] = source_terms(pkt[0, 0:8, :])
    products(0)
    send_densities()

    def look_up():
        each(1, NQ, lambda n: from_quarter(n, lists, lists_send, lists_recv).wait_recv())
        sub = lax.broadcasted_iota(jnp.int32, (8, LANES), 0)
        homes = []
        for group in range(PACKETS // 8):
            homes.append([])
            for t in range(halves):
                home = jnp.zeros((8, LANES), jnp.int32)
                for row in range(8):
                    dy, dz = OFFSETS[2 * (8 * group + row) + t]
                    home = jnp.where(sub == row, ys[dy] + zs[dz], home)
                homes[group].append(home)
        for j in range(NQ):
            for h in range(halves):
                cols = slice(h * LANES, (h + 1) * LANES)
                own = jnp.broadcast_to(lists[j, 0:1, cols], (8, LANES))
                place = jnp.broadcast_to(lists[j, 1:2, cols], (8, LANES))
                found = [jnp.zeros((8, LANES), F32) for _ in range(4)]
                for group in range(PACKETS // 8):
                    for t in range(halves):
                        hit = jnp.logical_and(own == homes[group][t], place // LANES == rhs)
                        for c in range(4):
                            table = pkt[8 * group : 8 * group + 8, 12 + c, t * LANES : (t + 1) * LANES]
                            value = jnp.take_along_axis(table, place % LANES, axis=1)
                            found[c] = found[c] + jnp.where(hit, value, 0.0)
                for c in range(4):
                    listed[2 * j + c % 2, c // 2 : c // 2 + 1, cols] = jnp.sum(found[c], 0, keepdims=True)
        each(1, 2 * NQ, lambda n: to_column(n, listed, listed_got, listed_send, listed_recv).start())

    def packet(p, now):
        then = 1 - now

        @pl.when(jnp.logical_and(p > 1, p <= EARLY // 2))
        def _():
            for half in range(2):
                arrival(p - 1, half, den_rows, den_recv).wait_recv()

        @pl.when(p == 1)
        def _():
            arrival(0, 1, den_rows, den_recv).wait_recv()
            acc[...] = jnp.zeros_like(acc)

        @pl.when(p + 1 < EARLY // 2)
        def _():
            for half in range(2):
                arrival(p + 1, half, geo_rows, pkt_recv).wait_recv()

        @pl.when(jnp.logical_and(p + 1 >= EARLY // 2, p < LIST_AT))
        def _():
            for half in range(2):
                arrival(p + 1, half, all_rows, pkt_recv).wait_recv()

        if now == LIST_AT % 2:

            @pl.when(p == LIST_AT)
            def _():
                for k in range(LIST_AT + 1, PACKETS):
                    for half in range(2):
                        arrival(k, half, all_rows, pkt_recv).wait_recv()
                look_up()

        @pl.when(p > 0)
        def _():
            left[...] = density_terms(p - 1)

        for j in range(NQ):
            apply(j, NQ * then + j)
            if j == NQ - 1:
                terms[...] = source_terms(pkt[jnp.minimum(p + 1, PACKETS - 1), 0:8, :])
            products(j + 1)
            pairs(j, NQ * now + j)

    def body(i, carry):
        packet(2 * i, 0)
        packet(2 * i + 1, 1)
        return carry

    lax.fori_loop(0, PACKETS // 2, body, 0)
    left[...] = density_terms(PACKETS - 1)
    for j in range(NQ):
        apply(j, NQ + j)
    for j in range(NQ):
        total = acc[j]
        far = total[0:4] + total[4:8]
        for r in range(2):
            part[2 * j + r] = jnp.concatenate([far[r : r + 1], far[2 + r : 3 + r]], 0)
    each(1, 2 * NQ, lambda n: to_column(n, part, part_got, part_send, part_recv).start())

    loads[6].wait()
    loads[7].wait()
    me = 2 * q + rhs
    listed_got[me] = listed[me]
    each(1, 2 * NQ, lambda n: from_column(n, listed, listed_got, listed_send, listed_recv).wait_recv())
    mine_listed = jnp.sum(listed_got[...], 0)
    near = [[], []]
    neighbours = index_hbm.shape[0]
    tables = [
        [
            jnp.broadcast_to(mine_listed[c : c + 1, t * LANES : (t + 1) * LANES], (8, LANES))
            for t in range(halves)
        ]
        for c in range(2)
    ]
    for h in range(halves):
        cols = slice(h * LANES, (h + 1) * LANES)
        sums = [jnp.zeros((8, LANES), F32) for _ in range(2)]
        for m in range(neighbours // 8):
            rows = slice(8 * m, 8 * m + 8)
            where_to = index_in[rows, cols]
            looked = []
            for c in range(2):
                value = jnp.zeros((8, LANES), F32)
                for t in range(halves):
                    found = jnp.take_along_axis(tables[c][t], where_to % LANES, axis=1)
                    value = jnp.where(where_to // LANES == t, found, value)
                looked.append(value)
            real, imag = coef_in[0, rows, cols], coef_in[1, rows, cols]
            sums[0] = sums[0] + (real * looked[0] - imag * looked[1])
            sums[1] = sums[1] + (real * looked[1] + imag * looked[0])
        for c in range(2):
            near[c].append(jnp.sum(sums[c], 0, keepdims=True))
    near = jnp.concatenate([jnp.concatenate(row, 1) for row in near], 0)

    part_got[me] = part[me]

    swap.wait_send()
    loop(1, EARLY, lambda n: sent(n, geo_rows, pkt_send).wait_send())
    loop(1, EARLY, lambda n: sent(n, den_rows, den_send).wait_send())
    loop(EARLY, BLOCKS, lambda n: sent(n, all_rows, pkt_send).wait_send())
    each(1, NQ, lambda n: to_quarter(n, tpos, tpos_send, tpos_recv).wait_send())
    each(1, NQ, lambda n: to_quarter(n, lists, lists_send, lists_recv).wait_send())
    each(1, 2 * NQ, lambda n: to_column(n, listed, listed_got, listed_send, listed_recv).wait_send())
    each(1, 2 * NQ, lambda n: to_column(n, part, part_got, part_send, part_recv).wait_send())
    each(1, 2 * NQ, lambda n: from_column(n, part, part_got, part_send, part_recv).wait_recv())
    out_ref[0] = 0.5 * density + near + jnp.sum(part_got[...], 0)


def on_device(
    positions, normal_angles, areas, densities, need_owner, need_slot, near_index, near_coef
):
    count = positions.shape[1]
    args = (
        positions,
        normal_angles,
        areas.reshape(1, count),
        densities,
        need_owner.reshape(1, count),
        need_slot.reshape(1, count),
        near_index,
        near_coef,
    )
    dma = pltpu.SemaphoreType.DMA
    return pl.pallas_call(
        kernel,
        out_shape=jax.ShapeDtypeStruct((1, 2, count), F32),
        in_specs=[pl.BlockSpec(memory_space=pl.ANY)] * 8,
        out_specs=pl.BlockSpec(memory_space=pltpu.VMEM),
        scratch_shapes=[pltpu.VMEM(arg.shape, arg.dtype) for arg in args]
        + [
            pltpu.VMEM((PACKETS, 16, count), F32),
            pltpu.VMEM((4, LANES), F32),
            pltpu.VMEM((4, LANES), F32),
            pltpu.VMEM((NQ, 3, count), F32),
            pltpu.VMEM((NQ, 2, count), jnp.int32),
            pltpu.VMEM((NQ, 32, count), BF16),
            pltpu.VMEM((2 * count, 32), BF16),
            pltpu.VMEM((8, 4 * count), BF16),
            pltpu.VMEM((2 * count, count), F32),
            pltpu.VMEM((2 * count, count), F32),
        ]
        + [pltpu.VMEM((4 * count, count), BF16)] * (2 * NQ)
        + [
            pltpu.VMEM((NQ, 8, count), F32),
            pltpu.VMEM((2 * NQ, 2, count), F32),
            pltpu.VMEM((2 * NQ, 2, count), F32),
            pltpu.VMEM((2 * NQ, 2, count), F32),
            pltpu.VMEM((2 * NQ, 2, count), F32),
            dma((8,)), dma, dma,
            dma((BLOCKS,)), dma((BLOCKS,)), dma((EARLY,)), dma((EARLY,)),
            dma((NQ,)), dma((NQ,)), dma((NQ,)), dma((NQ,)),
            dma((2 * NQ,)), dma((2 * NQ,)), dma((2 * NQ,)), dma((2 * NQ,)),
        ],
        compiler_params=pltpu.CompilerParams(collective_id=0, has_side_effects=True),
        name="field",
    )(*args)


def solution(mesh):
    in_specs = (
        P(None, "blk"),
        P(None, "blk"),
        P("blk"),
        P("rhs", None, "blk"),
        P("blk", None),
        P("blk"),
        P(None, "blk"),
        P(None, None, "blk"),
    )
    return jax.shard_map(
        on_device, mesh=mesh, in_specs=in_specs, out_specs=P("rhs", None, "blk"), check_vma=False
    )
```

```python
import math

import jax
import jax.numpy as jnp
from jax import lax
from jax.experimental import pallas as pl
from jax.experimental.pallas import tpu as pltpu
from jax.sharding import PartitionSpec as P

F32 = jnp.float32
BF16 = jnp.bfloat16
MESH = pl.DeviceIdType.MESH

WAVE = 8.0
SOFT = 0.1
TWO_PI = 2.0 * math.pi
TURNS = WAVE / TWO_PI
TURNS2 = TURNS * TURNS
KAPPA = 1.0 / TWO_PI

C0 = 2.221441438377396
C1 = -0.9135295479465378
C2 = 0.11267874257383814
C3 = -0.006494477491585805

NY, NZ, NQ = 4, 8, 4
BLOCKS = NY * NZ
PACKETS = BLOCKS // 2
EARLY = 8
CHUNK = 16
LIST_AT = 12
LANES = 128


def ring(d, n):
    return min(d, n - d)


OFFSETS = sorted(
    ((dy, dz) for dy in range(NY) for dz in range(NZ)),
    key=lambda o: (ring(o[0], NY) + ring(o[1], NZ), o),
)
HOPS = [ring(dy, NY) + ring(dz, NZ) for dy, dz in OFFSETS]
FARTHEST = max(HOPS)


def within(hops):
    return sum(h <= hops for h in HOPS)


def half_circle(turns):
    v = turns - jnp.round(turns)
    z = v * v
    s = v * (C0 + z * (C1 + z * (C2 + z * C3)))
    q = s * s
    w = 2.0 - q
    s2 = s * (w * lax.rsqrt(w))
    return 0.5 - s2 * s2, s2 * (1.0 - q)


def pair_kernel(turns2, facing):
    h = lax.rsqrt(turns2)
    cosine, sine = half_circle(turns2 * h)
    p = facing * (h * h)
    hk = h * KAPPA
    a = p * hk
    e = p + hk
    return a * cosine + e * sine, a * sine - e * cosine


def split3(x):
    hi = x.astype(BF16).astype(F32)
    rest = x - hi
    mid = rest.astype(BF16).astype(F32)
    return hi, mid, rest - mid


def split2(x):
    hi = x.astype(BF16)
    return hi, (x - hi.astype(F32)).astype(BF16)


def source_terms(geo):
    parts = split3(geo)
    count = geo.shape[1]
    row = lax.broadcasted_iota(jnp.int32, (4, count), 0)

    def stack(k):
        hi, mid, lo = (part[4 * k : 4 * k + 4] for part in parts)
        ones = jnp.where(row < 3, 1.0 if k == 0 else 0.0, 0.0)
        rows = [hi, mid, lo, hi, mid, hi, ones, jnp.zeros((4, count), F32)]
        return jnp.concatenate(rows, 0).T.astype(BF16)

    return jnp.concatenate([stack(0), stack(1)], 0)


def target_terms(pos):
    count = pos.shape[1]
    hi, mid, lo = split3(pos)
    square = split3(TURNS2 * jnp.sum(pos * pos, 0, keepdims=True))
    one = jnp.ones((1, count), F32)
    zero = jnp.zeros((1, count), F32)
    rows = [hi, one, hi, one, hi, one, mid, zero, mid, zero, lo, zero]
    rows += [square[0], square[1], square[2]] + [zero] * 5
    return jnp.concatenate(rows, 0).astype(BF16)


def kernel(
    pos_hbm, ang_hbm, area_hbm, den_hbm, owner_hbm, slot_hbm, index_hbm, coef_hbm, out_ref,
    pos_in, ang_in, area_in, den_in, owner_in, slot_in, index_in, coef_in,
    pkt, mine, other, tpos, lists, tf, terms, left, rf0, rf1, k0, k1, k2, k3, k4, k5, k6, k7, acc,
    listed, listed_got, part, part_got,
    in_sem, round_sem, swap_send, swap_recv, pkt_send, pkt_recv, den_send, den_recv,
    tpos_send, tpos_recv, lists_send, lists_recv, listed_send, listed_recv, part_send, part_recv,
):
    count = pos_hbm.shape[1]
    halves = count // LANES
    blk = lax.axis_index("blk")
    rhs = lax.axis_index("rhs")
    q = blk % NQ
    z = (blk // NQ) % NZ
    y = blk // (NQ * NZ)
    column_base = blk - q
    side = 1 - rhs
    zs = [lax.rem(z + d, NZ) * NQ + q for d in range(NZ)]
    ys = [lax.rem(y + d, NY) * (NZ * NQ) for d in range(NY)]
    qs = [lax.rem(q + d, NQ) for d in range(NQ)]

    def device(b, r):
        return {"blk": b, "rhs": r}

    def column(n):
        return qs[n // 2], (side if n % 2 else rhs)

    def plane(n):
        dy, dz = OFFSETS[n]
        return device(ys[(NY - dy) % NY] + zs[(NZ - dz) % NZ], rhs)

    barrier = pltpu.get_barrier_semaphore()
    near = within(1)
    for n in range(1, near):
        pl.semaphore_signal(barrier, inc=1, device_id=plane(n), device_id_type=MESH)
    for n in range(1, 2 * NQ):
        cq, cr = column(n)
        pl.semaphore_signal(
            barrier, inc=1, device_id=device(column_base + cq, cr), device_id_type=MESH
        )

    loads = [
        pltpu.make_async_copy(src, dst, in_sem.at[n])
        for n, (src, dst) in enumerate(
            [
                (pos_hbm, pos_in), (ang_hbm, ang_in), (area_hbm, area_in), (den_hbm, den_in),
                (owner_hbm, owner_in), (slot_hbm, slot_in), (index_hbm, index_in), (coef_hbm, coef_in),
            ]
        )
    ]
    for load in loads:
        load.start()
    for load in loads[:6]:
        load.wait()

    def own_half(v):
        return jnp.where(rhs == 0, v[:, 0:LANES], v[:, LANES : 2 * LANES])

    def other_half(v):
        return jnp.where(rhs == 0, v[:, LANES : 2 * LANES], v[:, 0:LANES])

    pos = pos_in[...]
    tpos[q] = pos
    lists[q] = jnp.concatenate([owner_in[...], slot_in[...]], 0)
    cosines, sines = half_circle(ang_in[...] * KAPPA)
    cosines = 2.0 * cosines
    sines = 2.0 * sines
    normal = jnp.concatenate(
        [cosines[0:1] * cosines[1:2], sines[0:1] * cosines[1:2], sines[1:2]], 0
    )
    weight = area_in[...] * (TURNS / math.sqrt(count * BLOCKS * NQ))
    density = den_in[0]
    sources = jnp.concatenate([density * weight, density], 0)
    mine[...] = other_half(sources)
    pkt[0, 0:8, 0:LANES] = own_half(
        jnp.concatenate(
            [
                (-2.0 * TURNS2) * pos,
                TURNS2 * (jnp.sum(pos * pos, 0, keepdims=True) + SOFT * SOFT),
                TURNS2 * normal,
                -TURNS2 * jnp.sum(pos * normal, 0, keepdims=True),
            ],
            0,
        )
    )

    pl.semaphore_wait(barrier, 2 * NQ - 1 + near - 1)

    swap = pltpu.make_async_remote_copy(
        src_ref=mine, dst_ref=other, send_sem=swap_send, recv_sem=swap_recv,
        device_id=device(blk, side), device_id_type=MESH,
    )

    def lanes_of(n):
        return pl.ds((n % 2) * LANES, LANES)

    def plane_copy(n, rows, send, recv):
        return pltpu.make_async_remote_copy(
            src_ref=pkt.at[0, rows, pl.ds(0, LANES)], dst_ref=pkt.at[n // 2, rows, lanes_of(n)],
            send_sem=send.at[n], recv_sem=recv.at[n],
            device_id=plane(n), device_id_type=MESH,
        )

    geo_rows, den_rows, all_rows = pl.ds(0, 8), pl.ds(8, 8), pl.ds(0, 16)

    def arrival(k, half, rows, recv):
        return pltpu.make_async_remote_copy(
            src_ref=pkt.at[0, rows, pl.ds(0, LANES)],
            dst_ref=pkt.at[k, rows, pl.ds(half * LANES, LANES)],
            send_sem=swap_send, recv_sem=recv.at[2 * k + half],
            device_id=device(blk, side), device_id_type=MESH,
        )

    def sent(n, rows, send):
        return pltpu.make_async_remote_copy(
            src_ref=pkt.at[0, rows, pl.ds(0, LANES)], dst_ref=pkt.at[0, rows, pl.ds(0, LANES)],
            send_sem=send.at[n], recv_sem=swap_recv,
            device_id=device(blk, side), device_id_type=MESH,
        )

    def to_quarter(n, src, send, recv):
        return pltpu.make_async_remote_copy(
            src_ref=src.at[q], dst_ref=src.at[q], send_sem=send.at[n], recv_sem=recv.at[q],
            device_id=device(column_base + qs[n], rhs), device_id_type=MESH,
        )

    def from_quarter(n, src, send, recv):
        return pltpu.make_async_remote_copy(
            src_ref=src.at[q], dst_ref=src.at[qs[n]], send_sem=send.at[n], recv_sem=recv.at[qs[n]],
            device_id=device(column_base + qs[n], rhs), device_id_type=MESH,
        )

    def to_column(n, src, dst, send, recv):
        cq, cr = column(n)
        return pltpu.make_async_remote_copy(
            src_ref=src.at[2 * cq + cr], dst_ref=dst.at[2 * q + rhs],
            send_sem=send.at[n], recv_sem=recv.at[2 * q + rhs],
            device_id=device(column_base + cq, cr), device_id_type=MESH,
        )

    def from_column(n, src, dst, send, recv):
        cq, cr = column(n)
        return pltpu.make_async_remote_copy(
            src_ref=src.at[2 * cq + cr], dst_ref=dst.at[2 * cq + cr],
            send_sem=send.at[n], recv_sem=recv.at[2 * cq + cr],
            device_id=device(column_base + cq, cr), device_id_type=MESH,
        )

    def each(first, last, act):
        for n in range(first, last):
            act(n)

    def loop(first, last, act):
        def step(n, carry):
            act(n)
            return carry

        lax.fori_loop(first, last, step, 0)

    def tell(r):
        for n in range(1, near):
            pl.semaphore_signal(round_sem.at[r], inc=1, device_id=plane(n), device_id_type=MESH)

    def hear(r):
        pl.semaphore_wait(round_sem.at[r], near - 1)
        if r < FARTHEST:
            tell(r + 1)

    swap.start()
    tell(2)
    each(1, NQ, lambda n: to_quarter(n, tpos, tpos_send, tpos_recv).start())
    each(1, near, lambda n: plane_copy(n, geo_rows, pkt_send, pkt_recv).start())
    each(1, NQ, lambda n: to_quarter(n, lists, lists_send, lists_recv).start())

    def send_densities():
        swap.wait_recv()
        a = own_half(sources)
        b = other[...]
        first = jnp.where(rhs == 0, a, b)
        second = jnp.where(rhs == 0, b, a)
        pkt[0, 8:16, 0:LANES] = jnp.concatenate(
            [first[0:1], second[0:1], first[1:2], second[1:2], first[2:3], second[2:3], first[3:4], second[3:4]], 0
        )
        each(1, EARLY, lambda n: plane_copy(n, den_rows, den_send, den_recv).start())
        each(EARLY, within(2), lambda n: plane_copy(n, all_rows, pkt_send, pkt_recv).start())

    hear(2)
    each(near, EARLY, lambda n: plane_copy(n, geo_rows, pkt_send, pkt_recv).start())
    each(1, NQ, lambda n: from_quarter(n, tpos, tpos_send, tpos_recv).wait_recv())
    for j in range(NQ):
        tf[j] = target_terms(tpos[j])
    arrival(0, 1, geo_rows, pkt_recv).wait_recv()

    rf = (rf0, rf1)
    kk = (k0, k1, k2, k3, k4, k5, k6, k7)

    def products(j):
        for half in range(2):
            rows = slice(half * count, (half + 1) * count)
            rf[j % 2][rows] = jnp.dot(terms[rows], tf[j % NQ], preferred_element_type=F32)

    def pairs(j, b):
        for c in range(count // CHUNK):
            rows = slice(c * CHUNK, (c + 1) * CHUNK)
            real, imag = pair_kernel(
                rf[j % 2][rows], rf[j % 2][count + c * CHUNK : count + (c + 1) * CHUNK]
            )
            for n, piece in enumerate(split2(real) + split2(imag)):
                kk[b][n * count + c * CHUNK : n * count + (c + 1) * CHUNK] = piece

    def apply(j, b):
        acc[j] += jnp.dot(left[...], kk[b][...], preferred_element_type=F32)

    def density_terms(p):
        rows = pkt[p, 8:12, :]
        turned = jnp.concatenate([-rows[2:4], rows[0:2]], 0)

        def both(v):
            hi = v.astype(BF16).astype(F32)
            return jnp.concatenate([hi, v - hi], 0).astype(BF16)

        real, imag = both(rows), both(turned)
        return jnp.concatenate([real, real, imag, imag], 1)

    terms[...] = source_terms(pkt[0, 0:8, :])
    products(0)
    send_densities()

    def look_up():
        each(1, NQ, lambda n: from_quarter(n, lists, lists_send, lists_recv).wait_recv())
        sub = lax.broadcasted_iota(jnp.int32, (8, LANES), 0)
        homes = []
        for group in range(PACKETS // 8):
            homes.append([])
            for t in range(halves):
                home = jnp.zeros((8, LANES), jnp.int32)
                for row in range(8):
                    dy, dz = OFFSETS[2 * (8 * group + row) + t]
                    home = jnp.where(sub == row, ys[dy] + zs[dz], home)
                homes[group].append(home)
        for j in range(NQ):
            for h in range(halves):
                cols = slice(h * LANES, (h + 1) * LANES)
                own = jnp.broadcast_to(lists[j, 0:1, cols], (8, LANES))
                place = jnp.broadcast_to(lists[j, 1:2, cols], (8, LANES))
                found = [jnp.zeros((8, LANES), F32) for _ in range(4)]
                for group in range(PACKETS // 8):
                    for t in range(halves):
                        hit = jnp.logical_and(own == homes[group][t], place // LANES == rhs)
                        for c in range(4):
                            table = pkt[8 * group : 8 * group + 8, 12 + c, t * LANES : (t + 1) * LANES]
                            value = jnp.take_along_axis(table, place % LANES, axis=1)
                            found[c] = found[c] + jnp.where(hit, value, 0.0)
                for c in range(4):
                    listed[2 * j + c % 2, c // 2 : c // 2 + 1, cols] = jnp.sum(found[c], 0, keepdims=True)
        each(1, 2 * NQ, lambda n: to_column(n, listed, listed_got, listed_send, listed_recv).start())

    def packet(p, now):
        then = 1 - now

        @pl.when(jnp.logical_and(p > 1, p <= EARLY // 2))
        def _():
            for half in range(2):
                arrival(p - 1, half, den_rows, den_recv).wait_recv()

        @pl.when(p == 1)
        def _():
            arrival(0, 1, den_rows, den_recv).wait_recv()
            acc[...] = jnp.zeros_like(acc)

        @pl.when(p + 1 < EARLY // 2)
        def _():
            for half in range(2):
                arrival(p + 1, half, geo_rows, pkt_recv).wait_recv()

        @pl.when(jnp.logical_and(p + 1 >= EARLY // 2, p < LIST_AT))
        def _():
            for half in range(2):
                arrival(p + 1, half, all_rows, pkt_recv).wait_recv()

        for r in range(3, FARTHEST + 1):
            if now == (r - 2) % 2:

                @pl.when(p == r - 2)
                def _():
                    hear(r)
                    each(
                        within(r - 1),
                        within(r),
                        lambda n: plane_copy(n, all_rows, pkt_send, pkt_recv).start(),
                    )

        if now == LIST_AT % 2:

            @pl.when(p == LIST_AT)
            def _():
                for k in range(LIST_AT + 1, PACKETS):
                    for half in range(2):
                        arrival(k, half, all_rows, pkt_recv).wait_recv()
                look_up()

        @pl.when(p > 0)
        def _():
            left[...] = density_terms(p - 1)

        for j in range(NQ):
            apply(j, NQ * then + j)
            if j == NQ - 1:
                terms[...] = source_terms(pkt[jnp.minimum(p + 1, PACKETS - 1), 0:8, :])
            products(j + 1)
            pairs(j, NQ * now + j)

    def body(i, carry):
        packet(2 * i, 0)
        packet(2 * i + 1, 1)
        return carry

    lax.fori_loop(0, PACKETS // 2, body, 0)
    left[...] = density_terms(PACKETS - 1)
    for j in range(NQ):
        apply(j, NQ + j)
    for j in range(NQ):
        total = acc[j]
        far = total[0:4] + total[4:8]
        for r in range(2):
            part[2 * j + r] = jnp.concatenate([far[r : r + 1], far[2 + r : 3 + r]], 0)
    each(1, 2 * NQ, lambda n: to_column(n, part, part_got, part_send, part_recv).start())

    loads[6].wait()
    loads[7].wait()
    me = 2 * q + rhs
    listed_got[me] = listed[me]
    each(1, 2 * NQ, lambda n: from_column(n, listed, listed_got, listed_send, listed_recv).wait_recv())
    mine_listed = jnp.sum(listed_got[...], 0)
    near = [[], []]
    neighbours = index_hbm.shape[0]
    tables = [
        [
            jnp.broadcast_to(mine_listed[c : c + 1, t * LANES : (t + 1) * LANES], (8, LANES))
            for t in range(halves)
        ]
        for c in range(2)
    ]
    for h in range(halves):
        cols = slice(h * LANES, (h + 1) * LANES)
        sums = [jnp.zeros((8, LANES), F32) for _ in range(2)]
        for m in range(neighbours // 8):
            rows = slice(8 * m, 8 * m + 8)
            where_to = index_in[rows, cols]
            looked = []
            for c in range(2):
                value = jnp.zeros((8, LANES), F32)
                for t in range(halves):
                    found = jnp.take_along_axis(tables[c][t], where_to % LANES, axis=1)
                    value = jnp.where(where_to // LANES == t, found, value)
                looked.append(value)
            real, imag = coef_in[0, rows, cols], coef_in[1, rows, cols]
            sums[0] = sums[0] + (real * looked[0] - imag * looked[1])
            sums[1] = sums[1] + (real * looked[1] + imag * looked[0])
        for c in range(2):
            near[c].append(jnp.sum(sums[c], 0, keepdims=True))
    near = jnp.concatenate([jnp.concatenate(row, 1) for row in near], 0)

    part_got[me] = part[me]

    swap.wait_send()
    loop(1, EARLY, lambda n: sent(n, geo_rows, pkt_send).wait_send())
    loop(1, EARLY, lambda n: sent(n, den_rows, den_send).wait_send())
    loop(EARLY, BLOCKS, lambda n: sent(n, all_rows, pkt_send).wait_send())
    each(1, NQ, lambda n: to_quarter(n, tpos, tpos_send, tpos_recv).wait_send())
    each(1, NQ, lambda n: to_quarter(n, lists, lists_send, lists_recv).wait_send())
    each(1, 2 * NQ, lambda n: to_column(n, listed, listed_got, listed_send, listed_recv).wait_send())
    each(1, 2 * NQ, lambda n: to_column(n, part, part_got, part_send, part_recv).wait_send())
    each(1, 2 * NQ, lambda n: from_column(n, part, part_got, part_send, part_recv).wait_recv())
    out_ref[0] = 0.5 * density + near + jnp.sum(part_got[...], 0)


def on_device(
    positions, normal_angles, areas, densities, need_owner, need_slot, near_index, near_coef
):
    count = positions.shape[1]
    args = (
        positions,
        normal_angles,
        areas.reshape(1, count),
        densities,
        need_owner.reshape(1, count),
        need_slot.reshape(1, count),
        near_index,
        near_coef,
    )
    dma = pltpu.SemaphoreType.DMA
    return pl.pallas_call(
        kernel,
        out_shape=jax.ShapeDtypeStruct((1, 2, count), F32),
        in_specs=[pl.BlockSpec(memory_space=pl.ANY)] * 8,
        out_specs=pl.BlockSpec(memory_space=pltpu.VMEM),
        scratch_shapes=[pltpu.VMEM(arg.shape, arg.dtype) for arg in args]
        + [
            pltpu.VMEM((PACKETS, 16, count), F32),
            pltpu.VMEM((4, LANES), F32),
            pltpu.VMEM((4, LANES), F32),
            pltpu.VMEM((NQ, 3, count), F32),
            pltpu.VMEM((NQ, 2, count), jnp.int32),
            pltpu.VMEM((NQ, 32, count), BF16),
            pltpu.VMEM((2 * count, 32), BF16),
            pltpu.VMEM((8, 4 * count), BF16),
            pltpu.VMEM((2 * count, count), F32),
            pltpu.VMEM((2 * count, count), F32),
        ]
        + [pltpu.VMEM((4 * count, count), BF16)] * (2 * NQ)
        + [
            pltpu.VMEM((NQ, 8, count), F32),
            pltpu.VMEM((2 * NQ, 2, count), F32),
            pltpu.VMEM((2 * NQ, 2, count), F32),
            pltpu.VMEM((2 * NQ, 2, count), F32),
            pltpu.VMEM((2 * NQ, 2, count), F32),
            dma((8,)), pltpu.SemaphoreType.REGULAR((FARTHEST + 1,)), dma, dma,
            dma((BLOCKS,)), dma((BLOCKS,)), dma((EARLY,)), dma((EARLY,)),
            dma((NQ,)), dma((NQ,)), dma((NQ,)), dma((NQ,)),
            dma((2 * NQ,)), dma((2 * NQ,)), dma((2 * NQ,)), dma((2 * NQ,)),
        ],
        compiler_params=pltpu.CompilerParams(collective_id=0, has_side_effects=True),
        name="field",
    )(*args)


def solution(mesh):
    in_specs = (
        P(None, "blk"),
        P(None, "blk"),
        P("blk"),
        P("rhs", None, "blk"),
        P("blk", None),
        P("blk"),
        P(None, "blk"),
        P(None, None, "blk"),
    )
    return jax.shard_map(
        on_device, mesh=mesh, in_specs=in_specs, out_specs=P("rhs", None, "blk"), check_vma=False
    )
```

```python
import math

import jax
import jax.numpy as jnp
from jax import lax
from jax.experimental import pallas as pl
from jax.experimental.pallas import tpu as pltpu
from jax.sharding import PartitionSpec as P

F32 = jnp.float32
BF16 = jnp.bfloat16
MESH = pl.DeviceIdType.MESH

WAVE = 8.0
SOFT = 0.1
TWO_PI = 2.0 * math.pi
TURNS = WAVE / TWO_PI
TURNS2 = TURNS * TURNS
KAPPA = 1.0 / TWO_PI

C0 = 2.221441438377396
C1 = -0.9135295479465378
C2 = 0.11267874257383814
C3 = -0.006494477491585805

NY, NZ, NQ = 4, 8, 4
BLOCKS = NY * NZ
PACKETS = BLOCKS // 2
EARLY = 8
CHUNK = 16
LIST_AT = 14
LANES = 128
ROUND_AT = {3: 2, 4: 4, 5: 7, 6: 9}


def ring(d, n):
    return min(d, n - d)


OFFSETS = sorted(
    ((dy, dz) for dy in range(NY) for dz in range(NZ)),
    key=lambda o: (ring(o[0], NY) + ring(o[1], NZ), o),
)
HOPS = [ring(dy, NY) + ring(dz, NZ) for dy, dz in OFFSETS]
FARTHEST = max(HOPS)


def within(hops):
    return sum(h <= hops for h in HOPS)


def half_circle(turns):
    v = turns - jnp.round(turns)
    z = v * v
    s = v * (C0 + z * (C1 + z * (C2 + z * C3)))
    q = s * s
    w = 2.0 - q
    s2 = s * (w * lax.rsqrt(w))
    return 0.5 - s2 * s2, s2 * (1.0 - q)


def pair_kernel(turns2, facing):
    h = lax.rsqrt(turns2)
    cosine, sine = half_circle(turns2 * h)
    p = facing * (h * h)
    hk = h * KAPPA
    a = p * hk
    e = p + hk
    return a * cosine + e * sine, a * sine - e * cosine


def split3(x):
    hi = x.astype(BF16).astype(F32)
    rest = x - hi
    mid = rest.astype(BF16).astype(F32)
    return hi, mid, rest - mid


def split2(x):
    hi = x.astype(BF16)
    return hi, (x - hi.astype(F32)).astype(BF16)


def source_terms(geo):
    parts = split3(geo)
    count = geo.shape[1]
    row = lax.broadcasted_iota(jnp.int32, (4, count), 0)

    def stack(k):
        hi, mid, lo = (part[4 * k : 4 * k + 4] for part in parts)
        ones = jnp.where(row < 3, 1.0 if k == 0 else 0.0, 0.0)
        rows = [hi, mid, lo, hi, mid, hi, ones, jnp.zeros((4, count), F32)]
        return jnp.concatenate(rows, 0).T.astype(BF16)

    return jnp.concatenate([stack(0), stack(1)], 0)


def target_terms(pos):
    count = pos.shape[1]
    hi, mid, lo = split3(pos)
    square = split3(TURNS2 * jnp.sum(pos * pos, 0, keepdims=True))
    one = jnp.ones((1, count), F32)
    zero = jnp.zeros((1, count), F32)
    rows = [hi, one, hi, one, hi, one, mid, zero, mid, zero, lo, zero]
    rows += [square[0], square[1], square[2]] + [zero] * 5
    return jnp.concatenate(rows, 0).astype(BF16)


def kernel(
    pos_hbm, ang_hbm, area_hbm, den_hbm, owner_hbm, slot_hbm, index_hbm, coef_hbm, out_ref,
    pos_in, ang_in, area_in, den_in, owner_in, slot_in, index_in, coef_in,
    pkt, mine, other, tpos, lists, tf, terms, left, rf0, rf1, k0, k1, k2, k3, k4, k5, k6, k7, acc,
    listed, listed_got, part, part_got,
    in_sem, round_sem, swap_send, swap_recv, pkt_send, pkt_recv, den_send, den_recv,
    tpos_send, tpos_recv, lists_send, lists_recv, listed_send, listed_recv, part_send, part_recv,
):
    count = pos_hbm.shape[1]
    halves = count // LANES
    blk = lax.axis_index("blk")
    rhs = lax.axis_index("rhs")
    q = blk % NQ
    z = (blk // NQ) % NZ
    y = blk // (NQ * NZ)
    column_base = blk - q
    side = 1 - rhs
    zs = [lax.rem(z + d, NZ) * NQ + q for d in range(NZ)]
    ys = [lax.rem(y + d, NY) * (NZ * NQ) for d in range(NY)]
    qs = [lax.rem(q + d, NQ) for d in range(NQ)]

    def device(b, r):
        return {"blk": b, "rhs": r}

    def column(n):
        return qs[n // 2], (side if n % 2 else rhs)

    def plane(n):
        dy, dz = OFFSETS[n]
        return device(ys[(NY - dy) % NY] + zs[(NZ - dz) % NZ], rhs)

    barrier = pltpu.get_barrier_semaphore()
    near = within(1)
    for n in range(1, near):
        pl.semaphore_signal(barrier, inc=1, device_id=plane(n), device_id_type=MESH)
    for n in range(1, 2 * NQ):
        cq, cr = column(n)
        pl.semaphore_signal(
            barrier, inc=1, device_id=device(column_base + cq, cr), device_id_type=MESH
        )

    loads = [
        pltpu.make_async_copy(src, dst, in_sem.at[n])
        for n, (src, dst) in enumerate(
            [
                (pos_hbm, pos_in), (ang_hbm, ang_in), (area_hbm, area_in), (den_hbm, den_in),
                (owner_hbm, owner_in), (slot_hbm, slot_in), (index_hbm, index_in), (coef_hbm, coef_in),
            ]
        )
    ]
    for load in loads:
        load.start()
    for load in loads[:6]:
        load.wait()

    def own_half(v):
        return jnp.where(rhs == 0, v[:, 0:LANES], v[:, LANES : 2 * LANES])

    def other_half(v):
        return jnp.where(rhs == 0, v[:, LANES : 2 * LANES], v[:, 0:LANES])

    pos = pos_in[...]
    tpos[q] = pos
    lists[q] = jnp.concatenate([owner_in[...], slot_in[...]], 0)
    cosines, sines = half_circle(ang_in[...] * KAPPA)
    cosines = 2.0 * cosines
    sines = 2.0 * sines
    normal = jnp.concatenate(
        [cosines[0:1] * cosines[1:2], sines[0:1] * cosines[1:2], sines[1:2]], 0
    )
    weight = area_in[...] * (TURNS / math.sqrt(count * BLOCKS * NQ))
    density = den_in[0]
    sources = jnp.concatenate([density * weight, density], 0)
    mine[...] = other_half(sources)
    pkt[0, 0:8, 0:LANES] = own_half(
        jnp.concatenate(
            [
                (-2.0 * TURNS2) * pos,
                TURNS2 * (jnp.sum(pos * pos, 0, keepdims=True) + SOFT * SOFT),
                TURNS2 * normal,
                -TURNS2 * jnp.sum(pos * normal, 0, keepdims=True),
            ],
            0,
        )
    )

    pl.semaphore_wait(barrier, 2 * NQ - 1 + near - 1)

    swap = pltpu.make_async_remote_copy(
        src_ref=mine, dst_ref=other, send_sem=swap_send, recv_sem=swap_recv,
        device_id=device(blk, side), device_id_type=MESH,
    )

    def lanes_of(n):
        return pl.ds((n % 2) * LANES, LANES)

    def plane_copy(n, rows, send, recv):
        return pltpu.make_async_remote_copy(
            src_ref=pkt.at[0, rows, pl.ds(0, LANES)], dst_ref=pkt.at[n // 2, rows, lanes_of(n)],
            send_sem=send.at[n], recv_sem=recv.at[n],
            device_id=plane(n), device_id_type=MESH,
        )

    geo_rows, den_rows, all_rows = pl.ds(0, 8), pl.ds(8, 8), pl.ds(0, 16)

    def arrival(k, half, rows, recv):
        return pltpu.make_async_remote_copy(
            src_ref=pkt.at[0, rows, pl.ds(0, LANES)],
            dst_ref=pkt.at[k, rows, pl.ds(half * LANES, LANES)],
            send_sem=swap_send, recv_sem=recv.at[2 * k + half],
            device_id=device(blk, side), device_id_type=MESH,
        )

    def sent(n, rows, send):
        return pltpu.make_async_remote_copy(
            src_ref=pkt.at[0, rows, pl.ds(0, LANES)], dst_ref=pkt.at[0, rows, pl.ds(0, LANES)],
            send_sem=send.at[n], recv_sem=swap_recv,
            device_id=device(blk, side), device_id_type=MESH,
        )

    def to_quarter(n, src, send, recv):
        return pltpu.make_async_remote_copy(
            src_ref=src.at[q], dst_ref=src.at[q], send_sem=send.at[n], recv_sem=recv.at[q],
            device_id=device(column_base + qs[n], rhs), device_id_type=MESH,
        )

    def from_quarter(n, src, send, recv):
        return pltpu.make_async_remote_copy(
            src_ref=src.at[q], dst_ref=src.at[qs[n]], send_sem=send.at[n], recv_sem=recv.at[qs[n]],
            device_id=device(column_base + qs[n], rhs), device_id_type=MESH,
        )

    def to_column(n, src, dst, send, recv):
        cq, cr = column(n)
        return pltpu.make_async_remote_copy(
            src_ref=src.at[2 * cq + cr], dst_ref=dst.at[2 * q + rhs],
            send_sem=send.at[n], recv_sem=recv.at[2 * q + rhs],
            device_id=device(column_base + cq, cr), device_id_type=MESH,
        )

    def from_column(n, src, dst, send, recv):
        cq, cr = column(n)
        return pltpu.make_async_remote_copy(
            src_ref=src.at[2 * cq + cr], dst_ref=dst.at[2 * cq + cr],
            send_sem=send.at[n], recv_sem=recv.at[2 * cq + cr],
            device_id=device(column_base + cq, cr), device_id_type=MESH,
        )

    def each(first, last, act):
        for n in range(first, last):
            act(n)

    def loop(first, last, act):
        def step(n, carry):
            act(n)
            return carry

        lax.fori_loop(first, last, step, 0)

    def tell(r):
        for n in range(1, near):
            pl.semaphore_signal(round_sem.at[r], inc=1, device_id=plane(n), device_id_type=MESH)

    def hear(r):
        pl.semaphore_wait(round_sem.at[r], near - 1)
        if r < FARTHEST:
            tell(r + 1)

    swap.start()
    tell(2)
    each(1, NQ, lambda n: to_quarter(n, tpos, tpos_send, tpos_recv).start())
    each(1, near, lambda n: plane_copy(n, geo_rows, pkt_send, pkt_recv).start())
    each(1, NQ, lambda n: to_quarter(n, lists, lists_send, lists_recv).start())

    def send_densities():
        swap.wait_recv()
        a = own_half(sources)
        b = other[...]
        first = jnp.where(rhs == 0, a, b)
        second = jnp.where(rhs == 0, b, a)
        pkt[0, 8:16, 0:LANES] = jnp.concatenate(
            [first[0:1], second[0:1], first[1:2], second[1:2], first[2:3], second[2:3], first[3:4], second[3:4]], 0
        )
        each(1, EARLY, lambda n: plane_copy(n, den_rows, den_send, den_recv).start())
        each(EARLY, within(2), lambda n: plane_copy(n, all_rows, pkt_send, pkt_recv).start())

    hear(2)
    each(near, EARLY, lambda n: plane_copy(n, geo_rows, pkt_send, pkt_recv).start())
    each(1, NQ, lambda n: from_quarter(n, tpos, tpos_send, tpos_recv).wait_recv())
    for j in range(NQ):
        tf[j] = target_terms(tpos[j])
    arrival(0, 1, geo_rows, pkt_recv).wait_recv()

    rf = (rf0, rf1)
    kk = (k0, k1, k2, k3, k4, k5, k6, k7)

    def products(j):
        for half in range(2):
            rows = slice(half * count, (half + 1) * count)
            rf[j % 2][rows] = jnp.dot(terms[rows], tf[j % NQ], preferred_element_type=F32)

    def pairs(j, b):
        for c in range(count // CHUNK):
            rows = slice(c * CHUNK, (c + 1) * CHUNK)
            real, imag = pair_kernel(
                rf[j % 2][rows], rf[j % 2][count + c * CHUNK : count + (c + 1) * CHUNK]
            )
            for n, piece in enumerate(split2(real) + split2(imag)):
                kk[b][n * count + c * CHUNK : n * count + (c + 1) * CHUNK] = piece

    def apply(j, b):
        acc[j] += jnp.dot(left[...], kk[b][...], preferred_element_type=F32)

    def density_terms(p):
        rows = pkt[p, 8:12, :]
        turned = jnp.concatenate([-rows[2:4], rows[0:2]], 0)

        def both(v):
            hi = v.astype(BF16).astype(F32)
            return jnp.concatenate([hi, v - hi], 0).astype(BF16)

        real, imag = both(rows), both(turned)
        return jnp.concatenate([real, real, imag, imag], 1)

    terms[...] = source_terms(pkt[0, 0:8, :])
    products(0)
    send_densities()

    def look_up():
        each(1, NQ, lambda n: from_quarter(n, lists, lists_send, lists_recv).wait_recv())
        sub = lax.broadcasted_iota(jnp.int32, (8, LANES), 0)
        homes = []
        for group in range(PACKETS // 8):
            homes.append([])
            for t in range(halves):
                home = jnp.zeros((8, LANES), jnp.int32)
                for row in range(8):
                    dy, dz = OFFSETS[2 * (8 * group + row) + t]
                    home = jnp.where(sub == row, ys[dy] + zs[dz], home)
                homes[group].append(home)
        for j in range(NQ):
            for h in range(halves):
                cols = slice(h * LANES, (h + 1) * LANES)
                own = jnp.broadcast_to(lists[j, 0:1, cols], (8, LANES))
                place = jnp.broadcast_to(lists[j, 1:2, cols], (8, LANES))
                found = [jnp.zeros((8, LANES), F32) for _ in range(4)]
                for group in range(PACKETS // 8):
                    for t in range(halves):
                        hit = jnp.logical_and(own == homes[group][t], place // LANES == rhs)
                        for c in range(4):
                            table = pkt[8 * group : 8 * group + 8, 12 + c, t * LANES : (t + 1) * LANES]
                            value = jnp.take_along_axis(table, place % LANES, axis=1)
                            found[c] = found[c] + jnp.where(hit, value, 0.0)
                for c in range(4):
                    listed[2 * j + c % 2, c // 2 : c // 2 + 1, cols] = jnp.sum(found[c], 0, keepdims=True)
        each(1, 2 * NQ, lambda n: to_column(n, listed, listed_got, listed_send, listed_recv).start())

    def packet(p, now):
        then = 1 - now

        @pl.when(jnp.logical_and(p > 1, p <= EARLY // 2))
        def _():
            for half in range(2):
                arrival(p - 1, half, den_rows, den_recv).wait_recv()

        @pl.when(p == 1)
        def _():
            arrival(0, 1, den_rows, den_recv).wait_recv()
            acc[...] = jnp.zeros_like(acc)

        @pl.when(p + 1 < EARLY // 2)
        def _():
            for half in range(2):
                arrival(p + 1, half, geo_rows, pkt_recv).wait_recv()

        @pl.when(jnp.logical_and(p + 1 >= EARLY // 2, p < LIST_AT))
        def _():
            for half in range(2):
                arrival(p + 1, half, all_rows, pkt_recv).wait_recv()

        for r in range(3, FARTHEST + 1):
            if now == ROUND_AT[r] % 2:

                @pl.when(p == ROUND_AT[r])
                def _():
                    hear(r)
                    each(
                        within(r - 1),
                        within(r),
                        lambda n: plane_copy(n, all_rows, pkt_send, pkt_recv).start(),
                    )

        if now == LIST_AT % 2:

            @pl.when(p == LIST_AT)
            def _():
                for k in range(LIST_AT + 1, PACKETS):
                    for half in range(2):
                        arrival(k, half, all_rows, pkt_recv).wait_recv()
                look_up()

        @pl.when(p > 0)
        def _():
            left[...] = density_terms(p - 1)

        for j in range(NQ):
            apply(j, NQ * then + j)
            if j == NQ - 1:
                terms[...] = source_terms(pkt[jnp.minimum(p + 1, PACKETS - 1), 0:8, :])
            products(j + 1)
            pairs(j, NQ * now + j)

    def body(i, carry):
        packet(2 * i, 0)
        packet(2 * i + 1, 1)
        return carry

    lax.fori_loop(0, PACKETS // 2, body, 0)
    left[...] = density_terms(PACKETS - 1)
    for j in range(NQ):
        apply(j, NQ + j)
    for j in range(NQ):
        total = acc[j]
        far = total[0:4] + total[4:8]
        for r in range(2):
            part[2 * j + r] = jnp.concatenate([far[r : r + 1], far[2 + r : 3 + r]], 0)
    each(1, 2 * NQ, lambda n: to_column(n, part, part_got, part_send, part_recv).start())

    loads[6].wait()
    loads[7].wait()
    me = 2 * q + rhs
    listed_got[me] = listed[me]
    each(1, 2 * NQ, lambda n: from_column(n, listed, listed_got, listed_send, listed_recv).wait_recv())
    mine_listed = jnp.sum(listed_got[...], 0)
    near = [[], []]
    neighbours = index_hbm.shape[0]
    tables = [
        [
            jnp.broadcast_to(mine_listed[c : c + 1, t * LANES : (t + 1) * LANES], (8, LANES))
            for t in range(halves)
        ]
        for c in range(2)
    ]
    for h in range(halves):
        cols = slice(h * LANES, (h + 1) * LANES)
        sums = [jnp.zeros((8, LANES), F32) for _ in range(2)]
        for m in range(neighbours // 8):
            rows = slice(8 * m, 8 * m + 8)
            where_to = index_in[rows, cols]
            looked = []
            for c in range(2):
                value = jnp.zeros((8, LANES), F32)
                for t in range(halves):
                    found = jnp.take_along_axis(tables[c][t], where_to % LANES, axis=1)
                    value = jnp.where(where_to // LANES == t, found, value)
                looked.append(value)
            real, imag = coef_in[0, rows, cols], coef_in[1, rows, cols]
            sums[0] = sums[0] + (real * looked[0] - imag * looked[1])
            sums[1] = sums[1] + (real * looked[1] + imag * looked[0])
        for c in range(2):
            near[c].append(jnp.sum(sums[c], 0, keepdims=True))
    near = jnp.concatenate([jnp.concatenate(row, 1) for row in near], 0)

    part_got[me] = part[me]

    swap.wait_send()
    loop(1, EARLY, lambda n: sent(n, geo_rows, pkt_send).wait_send())
    loop(1, EARLY, lambda n: sent(n, den_rows, den_send).wait_send())
    loop(EARLY, BLOCKS, lambda n: sent(n, all_rows, pkt_send).wait_send())
    each(1, NQ, lambda n: to_quarter(n, tpos, tpos_send, tpos_recv).wait_send())
    each(1, NQ, lambda n: to_quarter(n, lists, lists_send, lists_recv).wait_send())
    each(1, 2 * NQ, lambda n: to_column(n, listed, listed_got, listed_send, listed_recv).wait_send())
    each(1, 2 * NQ, lambda n: to_column(n, part, part_got, part_send, part_recv).wait_send())
    each(1, 2 * NQ, lambda n: from_column(n, part, part_got, part_send, part_recv).wait_recv())
    out_ref[0] = 0.5 * density + near + jnp.sum(part_got[...], 0)


def on_device(
    positions, normal_angles, areas, densities, need_owner, need_slot, near_index, near_coef
):
    count = positions.shape[1]
    args = (
        positions,
        normal_angles,
        areas.reshape(1, count),
        densities,
        need_owner.reshape(1, count),
        need_slot.reshape(1, count),
        near_index,
        near_coef,
    )
    dma = pltpu.SemaphoreType.DMA
    return pl.pallas_call(
        kernel,
        out_shape=jax.ShapeDtypeStruct((1, 2, count), F32),
        in_specs=[pl.BlockSpec(memory_space=pl.ANY)] * 8,
        out_specs=pl.BlockSpec(memory_space=pltpu.VMEM),
        scratch_shapes=[pltpu.VMEM(arg.shape, arg.dtype) for arg in args]
        + [
            pltpu.VMEM((PACKETS, 16, count), F32),
            pltpu.VMEM((4, LANES), F32),
            pltpu.VMEM((4, LANES), F32),
            pltpu.VMEM((NQ, 3, count), F32),
            pltpu.VMEM((NQ, 2, count), jnp.int32),
            pltpu.VMEM((NQ, 32, count), BF16),
            pltpu.VMEM((2 * count, 32), BF16),
            pltpu.VMEM((8, 4 * count), BF16),
            pltpu.VMEM((2 * count, count), F32),
            pltpu.VMEM((2 * count, count), F32),
        ]
        + [pltpu.VMEM((4 * count, count), BF16)] * (2 * NQ)
        + [
            pltpu.VMEM((NQ, 8, count), F32),
            pltpu.VMEM((2 * NQ, 2, count), F32),
            pltpu.VMEM((2 * NQ, 2, count), F32),
            pltpu.VMEM((2 * NQ, 2, count), F32),
            pltpu.VMEM((2 * NQ, 2, count), F32),
            dma((8,)), pltpu.SemaphoreType.REGULAR((FARTHEST + 1,)), dma, dma,
            dma((BLOCKS,)), dma((BLOCKS,)), dma((EARLY,)), dma((EARLY,)),
            dma((NQ,)), dma((NQ,)), dma((NQ,)), dma((NQ,)),
            dma((2 * NQ,)), dma((2 * NQ,)), dma((2 * NQ,)), dma((2 * NQ,)),
        ],
        compiler_params=pltpu.CompilerParams(collective_id=0, has_side_effects=True),
        name="field",
    )(*args)


def solution(mesh):
    in_specs = (
        P(None, "blk"),
        P(None, "blk"),
        P("blk"),
        P("rhs", None, "blk"),
        P("blk", None),
        P("blk"),
        P(None, "blk"),
        P(None, None, "blk"),
    )
    return jax.shard_map(
        on_device, mesh=mesh, in_specs=in_specs, out_specs=P("rhs", None, "blk"), check_vma=False
    )
```

```python
import math

import jax
import jax.numpy as jnp
from jax import lax
from jax.experimental import pallas as pl
from jax.experimental.pallas import tpu as pltpu
from jax.sharding import PartitionSpec as P

F32 = jnp.float32
BF16 = jnp.bfloat16
MESH = pl.DeviceIdType.MESH

WAVE = 8.0
SOFT = 0.1
TWO_PI = 2.0 * math.pi
TURNS = WAVE / TWO_PI
TURNS2 = TURNS * TURNS
KAPPA = 1.0 / TWO_PI

C0 = 2.221441438377396
C1 = -0.9135295479465378
C2 = 0.11267874257383814
C3 = -0.006494477491585805

NY, NZ, NQ = 4, 8, 4
BLOCKS = NY * NZ
PACKETS = BLOCKS // 2
EARLY = 8
CHUNK = 16
LIST_AT = 14
LANES = 128
ROUND_AT = {3: 2, 4: 4, 5: 7, 6: 9}


def ring(d, n):
    return min(d, n - d)


OFFSETS = sorted(
    ((dy, dz) for dy in range(NY) for dz in range(NZ)),
    key=lambda o: (ring(o[0], NY) + ring(o[1], NZ), o),
)
HOPS = [ring(dy, NY) + ring(dz, NZ) for dy, dz in OFFSETS]
FARTHEST = max(HOPS)


def within(hops):
    return sum(h <= hops for h in HOPS)


def half_circle(turns):
    v = turns - jnp.round(turns)
    z = v * v
    s = v * (C0 + z * (C1 + z * (C2 + z * C3)))
    q = s * s
    w = 2.0 - q
    s2 = s * (w * lax.rsqrt(w))
    return 0.5 - s2 * s2, s2 * (1.0 - q)


def pair_kernel(turns2, facing):
    h = lax.rsqrt(turns2)
    cosine, sine = half_circle(turns2 * h)
    p = facing * (h * h)
    hk = h * KAPPA
    a = p * hk
    e = p + hk
    return a * cosine + e * sine, a * sine - e * cosine


def split3(x):
    hi = x.astype(BF16).astype(F32)
    rest = x - hi
    mid = rest.astype(BF16).astype(F32)
    return hi, mid, rest - mid


def split2(x):
    hi = x.astype(BF16)
    return hi, (x - hi.astype(F32)).astype(BF16)


def source_terms(geo):
    parts = split3(geo)
    count = geo.shape[1]
    row = lax.broadcasted_iota(jnp.int32, (4, count), 0)

    def stack(k):
        hi, mid, lo = (part[4 * k : 4 * k + 4] for part in parts)
        ones = jnp.where(row < 3, 1.0 if k == 0 else 0.0, 0.0)
        rows = [hi, mid, lo, hi, mid, hi, ones, jnp.zeros((4, count), F32)]
        return jnp.concatenate(rows, 0).T.astype(BF16)

    return jnp.concatenate([stack(0), stack(1)], 0)


def target_terms(pos):
    count = pos.shape[1]
    hi, mid, lo = split3(pos)
    square = split3(TURNS2 * jnp.sum(pos * pos, 0, keepdims=True))
    one = jnp.ones((1, count), F32)
    zero = jnp.zeros((1, count), F32)
    rows = [hi, one, hi, one, hi, one, mid, zero, mid, zero, lo, zero]
    rows += [square[0], square[1], square[2]] + [zero] * 5
    return jnp.concatenate(rows, 0).astype(BF16)


def kernel(
    pos_hbm, ang_hbm, area_hbm, den_hbm, owner_hbm, slot_hbm, index_hbm, coef_hbm, out_ref,
    pos_in, ang_in, area_in, den_in, owner_in, slot_in, index_in, coef_in,
    pkt, mine, other, tpos, lists, tf, terms, left, rf0, rf1, k0, k1, k2, k3, k4, k5, k6, k7, acc,
    listed, listed_got, part, part_got,
    in_sem, round_sem, swap_send, swap_recv, pkt_send, pkt_recv, den_send, den_recv,
    tpos_send, tpos_recv, lists_send, lists_recv, listed_send, listed_recv, part_send, part_recv,
):
    count = pos_hbm.shape[1]
    halves = count // LANES
    blk = lax.axis_index("blk")
    rhs = lax.axis_index("rhs")
    q = blk % NQ
    z = (blk // NQ) % NZ
    y = blk // (NQ * NZ)
    column_base = blk - q
    side = 1 - rhs
    zs = [lax.rem(z + d, NZ) * NQ + q for d in range(NZ)]
    ys = [lax.rem(y + d, NY) * (NZ * NQ) for d in range(NY)]
    qs = [lax.rem(q + d, NQ) for d in range(NQ)]

    def device(b, r):
        return {"blk": b, "rhs": r}

    def column(n):
        return qs[n // 2], (side if n % 2 else rhs)

    def plane(n):
        dy, dz = OFFSETS[n]
        return device(ys[(NY - dy) % NY] + zs[(NZ - dz) % NZ], rhs)

    barrier = pltpu.get_barrier_semaphore()
    near = within(1)
    for n in range(1, near):
        pl.semaphore_signal(barrier, inc=1, device_id=plane(n), device_id_type=MESH)
    for n in range(1, 2 * NQ):
        cq, cr = column(n)
        pl.semaphore_signal(
            barrier, inc=1, device_id=device(column_base + cq, cr), device_id_type=MESH
        )

    loads = [
        pltpu.make_async_copy(src, dst, in_sem.at[n])
        for n, (src, dst) in enumerate(
            [
                (pos_hbm, pos_in), (ang_hbm, ang_in), (area_hbm, area_in), (den_hbm, den_in),
                (owner_hbm, owner_in), (slot_hbm, slot_in), (index_hbm, index_in), (coef_hbm, coef_in),
            ]
        )
    ]
    for load in loads:
        load.start()
    for load in loads[:6]:
        load.wait()

    def own_half(v):
        return jnp.where(rhs == 0, v[:, 0:LANES], v[:, LANES : 2 * LANES])

    def other_half(v):
        return jnp.where(rhs == 0, v[:, LANES : 2 * LANES], v[:, 0:LANES])

    pos = pos_in[...]
    tpos[q] = pos
    lists[q] = jnp.concatenate([owner_in[...], slot_in[...]], 0)
    cosines, sines = half_circle(ang_in[...] * KAPPA)
    cosines = 2.0 * cosines
    sines = 2.0 * sines
    normal = jnp.concatenate(
        [cosines[0:1] * cosines[1:2], sines[0:1] * cosines[1:2], sines[1:2]], 0
    )
    weight = area_in[...] * (TURNS / math.sqrt(count * BLOCKS * NQ))
    density = den_in[0]
    sources = jnp.concatenate([density * weight, density], 0)
    mine[...] = other_half(sources)
    pkt[1, 0:8, 0:LANES] = own_half(
        jnp.concatenate(
            [
                (-2.0 * TURNS2) * pos,
                TURNS2 * (jnp.sum(pos * pos, 0, keepdims=True) + SOFT * SOFT),
                TURNS2 * normal,
                -TURNS2 * jnp.sum(pos * normal, 0, keepdims=True),
            ],
            0,
        )
    )

    pl.semaphore_wait(barrier, 2 * NQ - 1 + near - 1)

    swap = pltpu.make_async_remote_copy(
        src_ref=mine, dst_ref=other, send_sem=swap_send, recv_sem=swap_recv,
        device_id=device(blk, side), device_id_type=MESH,
    )

    def lanes_of(n):
        return pl.ds((n % 2) * LANES, LANES)

    def plane_copy(n, rows, send, recv):
        return pltpu.make_async_remote_copy(
            src_ref=pkt.at[1, rows, pl.ds(0, LANES)], dst_ref=pkt.at[n // 2 + 1, rows, lanes_of(n)],
            send_sem=send.at[n], recv_sem=recv.at[n],
            device_id=plane(n), device_id_type=MESH,
        )

    geo_rows, den_rows, all_rows = pl.ds(0, 8), pl.ds(8, 8), pl.ds(0, 16)

    def arrival(k, half, rows, recv):
        return pltpu.make_async_remote_copy(
            src_ref=pkt.at[1, rows, pl.ds(0, LANES)],
            dst_ref=pkt.at[k + 1, rows, pl.ds(half * LANES, LANES)],
            send_sem=swap_send, recv_sem=recv.at[2 * k + half],
            device_id=device(blk, side), device_id_type=MESH,
        )

    def sent(n, rows, send):
        return pltpu.make_async_remote_copy(
            src_ref=pkt.at[1, rows, pl.ds(0, LANES)], dst_ref=pkt.at[1, rows, pl.ds(0, LANES)],
            send_sem=send.at[n], recv_sem=swap_recv,
            device_id=device(blk, side), device_id_type=MESH,
        )

    def to_quarter(n, src, send, recv):
        return pltpu.make_async_remote_copy(
            src_ref=src.at[q], dst_ref=src.at[q], send_sem=send.at[n], recv_sem=recv.at[q],
            device_id=device(column_base + qs[n], rhs), device_id_type=MESH,
        )

    def from_quarter(n, src, send, recv):
        return pltpu.make_async_remote_copy(
            src_ref=src.at[q], dst_ref=src.at[qs[n]], send_sem=send.at[n], recv_sem=recv.at[qs[n]],
            device_id=device(column_base + qs[n], rhs), device_id_type=MESH,
        )

    def to_column(n, src, dst, send, recv):
        cq, cr = column(n)
        return pltpu.make_async_remote_copy(
            src_ref=src.at[2 * cq + cr], dst_ref=dst.at[2 * q + rhs],
            send_sem=send.at[n], recv_sem=recv.at[2 * q + rhs],
            device_id=device(column_base + cq, cr), device_id_type=MESH,
        )

    def from_column(n, src, dst, send, recv):
        cq, cr = column(n)
        return pltpu.make_async_remote_copy(
            src_ref=src.at[2 * cq + cr], dst_ref=dst.at[2 * cq + cr],
            send_sem=send.at[n], recv_sem=recv.at[2 * cq + cr],
            device_id=device(column_base + cq, cr), device_id_type=MESH,
        )

    def each(first, last, act):
        for n in range(first, last):
            act(n)

    def loop(first, last, act):
        def step(n, carry):
            act(n)
            return carry

        lax.fori_loop(first, last, step, 0)

    def tell(r):
        for n in range(1, near):
            pl.semaphore_signal(round_sem.at[r], inc=1, device_id=plane(n), device_id_type=MESH)

    def hear(r):
        pl.semaphore_wait(round_sem.at[r], near - 1)
        if r < FARTHEST:
            tell(r + 1)

    swap.start()
    tell(2)
    each(1, NQ, lambda n: to_quarter(n, tpos, tpos_send, tpos_recv).start())
    each(1, near, lambda n: plane_copy(n, geo_rows, pkt_send, pkt_recv).start())
    each(1, NQ, lambda n: to_quarter(n, lists, lists_send, lists_recv).start())

    def send_densities():
        swap.wait_recv()
        a = own_half(sources)
        b = other[...]
        first = jnp.where(rhs == 0, a, b)
        second = jnp.where(rhs == 0, b, a)
        pkt[1, 8:16, 0:LANES] = jnp.concatenate(
            [first[0:1], second[0:1], first[1:2], second[1:2], first[2:3], second[2:3], first[3:4], second[3:4]], 0
        )
        each(1, EARLY, lambda n: plane_copy(n, den_rows, den_send, den_recv).start())
        each(EARLY, within(2), lambda n: plane_copy(n, all_rows, pkt_send, pkt_recv).start())

    hear(2)
    each(near, EARLY, lambda n: plane_copy(n, geo_rows, pkt_send, pkt_recv).start())
    each(1, NQ, lambda n: from_quarter(n, tpos, tpos_send, tpos_recv).wait_recv())
    for j in range(NQ):
        tf[j] = target_terms(tpos[j])
    arrival(0, 1, geo_rows, pkt_recv).wait_recv()

    rf = (rf0, rf1)
    kk = (k0, k1, k2, k3, k4, k5, k6, k7)

    def products(j):
        for half in range(2):
            rows = slice(half * count, (half + 1) * count)
            rf[j % 2][rows] = jnp.dot(terms[rows], tf[j % NQ], preferred_element_type=F32)

    def pairs(j, b):
        for c in range(count // CHUNK):
            rows = slice(c * CHUNK, (c + 1) * CHUNK)
            real, imag = pair_kernel(
                rf[j % 2][rows], rf[j % 2][count + c * CHUNK : count + (c + 1) * CHUNK]
            )
            for n, piece in enumerate(split2(real) + split2(imag)):
                kk[b][n * count + c * CHUNK : n * count + (c + 1) * CHUNK] = piece

    def apply(j, b):
        acc[j] += jnp.dot(left[...], kk[b][...], preferred_element_type=F32)

    def density_terms(p):
        rows = pkt[p + 1, 8:12, :]
        turned = jnp.concatenate([-rows[2:4], rows[0:2]], 0)

        def both(v):
            hi = v.astype(BF16).astype(F32)
            return jnp.concatenate([hi, v - hi], 0).astype(BF16)

        real, imag = both(rows), both(turned)
        return jnp.concatenate([real, real, imag, imag], 1)

    terms[...] = source_terms(pkt[1, 0:8, :])
    products(0)
    send_densities()

    def look_up():
        each(1, NQ, lambda n: from_quarter(n, lists, lists_send, lists_recv).wait_recv())
        sub = lax.broadcasted_iota(jnp.int32, (8, LANES), 0)
        homes = []
        for group in range(PACKETS // 8):
            homes.append([])
            for t in range(halves):
                home = jnp.zeros((8, LANES), jnp.int32)
                for row in range(8):
                    dy, dz = OFFSETS[2 * (8 * group + row) + t]
                    home = jnp.where(sub == row, ys[dy] + zs[dz], home)
                homes[group].append(home)
        for j in range(NQ):
            for h in range(halves):
                cols = slice(h * LANES, (h + 1) * LANES)
                own = jnp.broadcast_to(lists[j, 0:1, cols], (8, LANES))
                place = jnp.broadcast_to(lists[j, 1:2, cols], (8, LANES))
                found = [jnp.zeros((8, LANES), F32) for _ in range(4)]
                for group in range(PACKETS // 8):
                    for t in range(halves):
                        hit = jnp.logical_and(own == homes[group][t], place // LANES == rhs)
                        for c in range(4):
                            table = pkt[8 * group + 1 : 8 * group + 9, 12 + c, t * LANES : (t + 1) * LANES]
                            value = jnp.take_along_axis(table, place % LANES, axis=1)
                            found[c] = found[c] + jnp.where(hit, value, 0.0)
                for c in range(4):
                    listed[2 * j + c % 2, c // 2 : c // 2 + 1, cols] = jnp.sum(found[c], 0, keepdims=True)
        each(1, 2 * NQ, lambda n: to_column(n, listed, listed_got, listed_send, listed_recv).start())

    def packet(p, now):
        then = 1 - now

        @pl.when(jnp.logical_and(p > 1, p <= EARLY // 2))
        def _():
            for half in range(2):
                arrival(p - 1, half, den_rows, den_recv).wait_recv()

        @pl.when(p == 1)
        def _():
            arrival(0, 1, den_rows, den_recv).wait_recv()
            acc[...] = jnp.zeros_like(acc)

        @pl.when(p + 1 < EARLY // 2)
        def _():
            for half in range(2):
                arrival(p + 1, half, geo_rows, pkt_recv).wait_recv()

        @pl.when(jnp.logical_and(p + 1 >= EARLY // 2, p < LIST_AT))
        def _():
            for half in range(2):
                arrival(p + 1, half, all_rows, pkt_recv).wait_recv()

        for r in range(3, FARTHEST + 1):
            if now == ROUND_AT[r] % 2:

                @pl.when(p == ROUND_AT[r])
                def _():
                    hear(r)
                    each(
                        within(r - 1),
                        within(r),
                        lambda n: plane_copy(n, all_rows, pkt_send, pkt_recv).start(),
                    )

        if now == LIST_AT % 2:

            @pl.when(p == LIST_AT)
            def _():
                for k in range(LIST_AT + 1, PACKETS):
                    for half in range(2):
                        arrival(k, half, all_rows, pkt_recv).wait_recv()
                look_up()

        left[...] = density_terms(p - 1)
        for j in range(NQ):
            apply(j, NQ * then + j)
            if j == NQ - 1:
                terms[...] = source_terms(pkt[jnp.minimum(p + 2, PACKETS), 0:8, :])
            products(j + 1)
            pairs(j, NQ * now + j)

    def body(i, carry):
        packet(2 * i, 0)
        packet(2 * i + 1, 1)
        return carry

    lax.fori_loop(0, PACKETS // 2, body, 0)
    left[...] = density_terms(PACKETS - 1)
    for j in range(NQ):
        apply(j, NQ + j)
    for j in range(NQ):
        total = acc[j]
        far = total[0:4] + total[4:8]
        for r in range(2):
            part[2 * j + r] = jnp.concatenate([far[r : r + 1], far[2 + r : 3 + r]], 0)
    each(1, 2 * NQ, lambda n: to_column(n, part, part_got, part_send, part_recv).start())

    loads[6].wait()
    loads[7].wait()
    me = 2 * q + rhs
    listed_got[me] = listed[me]
    each(1, 2 * NQ, lambda n: from_column(n, listed, listed_got, listed_send, listed_recv).wait_recv())
    mine_listed = jnp.sum(listed_got[...], 0)
    near = [[], []]
    neighbours = index_hbm.shape[0]
    tables = [
        [
            jnp.broadcast_to(mine_listed[c : c + 1, t * LANES : (t + 1) * LANES], (8, LANES))
            for t in range(halves)
        ]
        for c in range(2)
    ]
    for h in range(halves):
        cols = slice(h * LANES, (h + 1) * LANES)
        sums = [jnp.zeros((8, LANES), F32) for _ in range(2)]
        for m in range(neighbours // 8):
            rows = slice(8 * m, 8 * m + 8)
            where_to = index_in[rows, cols]
            looked = []
            for c in range(2):
                value = jnp.zeros((8, LANES), F32)
                for t in range(halves):
                    found = jnp.take_along_axis(tables[c][t], where_to % LANES, axis=1)
                    value = jnp.where(where_to // LANES == t, found, value)
                looked.append(value)
            real, imag = coef_in[0, rows, cols], coef_in[1, rows, cols]
            sums[0] = sums[0] + (real * looked[0] - imag * looked[1])
            sums[1] = sums[1] + (real * looked[1] + imag * looked[0])
        for c in range(2):
            near[c].append(jnp.sum(sums[c], 0, keepdims=True))
    near = jnp.concatenate([jnp.concatenate(row, 1) for row in near], 0)

    part_got[me] = part[me]

    swap.wait_send()
    loop(1, EARLY, lambda n: sent(n, geo_rows, pkt_send).wait_send())
    loop(1, EARLY, lambda n: sent(n, den_rows, den_send).wait_send())
    loop(EARLY, BLOCKS, lambda n: sent(n, all_rows, pkt_send).wait_send())
    each(1, NQ, lambda n: to_quarter(n, tpos, tpos_send, tpos_recv).wait_send())
    each(1, NQ, lambda n: to_quarter(n, lists, lists_send, lists_recv).wait_send())
    each(1, 2 * NQ, lambda n: to_column(n, listed, listed_got, listed_send, listed_recv).wait_send())
    each(1, 2 * NQ, lambda n: to_column(n, part, part_got, part_send, part_recv).wait_send())
    each(1, 2 * NQ, lambda n: from_column(n, part, part_got, part_send, part_recv).wait_recv())
    out_ref[0] = 0.5 * density + near + jnp.sum(part_got[...], 0)


def on_device(
    positions, normal_angles, areas, densities, need_owner, need_slot, near_index, near_coef
):
    count = positions.shape[1]
    args = (
        positions,
        normal_angles,
        areas.reshape(1, count),
        densities,
        need_owner.reshape(1, count),
        need_slot.reshape(1, count),
        near_index,
        near_coef,
    )
    dma = pltpu.SemaphoreType.DMA
    return pl.pallas_call(
        kernel,
        out_shape=jax.ShapeDtypeStruct((1, 2, count), F32),
        in_specs=[pl.BlockSpec(memory_space=pl.ANY)] * 8,
        out_specs=pl.BlockSpec(memory_space=pltpu.VMEM),
        scratch_shapes=[pltpu.VMEM(arg.shape, arg.dtype) for arg in args]
        + [
            pltpu.VMEM((PACKETS + 1, 16, count), F32),
            pltpu.VMEM((4, LANES), F32),
            pltpu.VMEM((4, LANES), F32),
            pltpu.VMEM((NQ, 3, count), F32),
            pltpu.VMEM((NQ, 2, count), jnp.int32),
            pltpu.VMEM((NQ, 32, count), BF16),
            pltpu.VMEM((2 * count, 32), BF16),
            pltpu.VMEM((8, 4 * count), BF16),
            pltpu.VMEM((2 * count, count), F32),
            pltpu.VMEM((2 * count, count), F32),
        ]
        + [pltpu.VMEM((4 * count, count), BF16)] * (2 * NQ)
        + [
            pltpu.VMEM((NQ, 8, count), F32),
            pltpu.VMEM((2 * NQ, 2, count), F32),
            pltpu.VMEM((2 * NQ, 2, count), F32),
            pltpu.VMEM((2 * NQ, 2, count), F32),
            pltpu.VMEM((2 * NQ, 2, count), F32),
            dma((8,)), pltpu.SemaphoreType.REGULAR((FARTHEST + 1,)), dma, dma,
            dma((BLOCKS,)), dma((BLOCKS,)), dma((EARLY,)), dma((EARLY,)),
            dma((NQ,)), dma((NQ,)), dma((NQ,)), dma((NQ,)),
            dma((2 * NQ,)), dma((2 * NQ,)), dma((2 * NQ,)), dma((2 * NQ,)),
        ],
        compiler_params=pltpu.CompilerParams(collective_id=0, has_side_effects=True),
        name="field",
    )(*args)


def solution(mesh):
    in_specs = (
        P(None, "blk"),
        P(None, "blk"),
        P("blk"),
        P("rhs", None, "blk"),
        P("blk", None),
        P("blk"),
        P(None, "blk"),
        P(None, None, "blk"),
    )
    return jax.shard_map(
        on_device, mesh=mesh, in_specs=in_specs, out_specs=P("rhs", None, "blk"), check_vma=False
    )
```

```python
import math

import jax
import jax.numpy as jnp
from jax import lax
from jax.experimental import pallas as pl
from jax.experimental.pallas import tpu as pltpu
from jax.sharding import PartitionSpec as P

F32 = jnp.float32
BF16 = jnp.bfloat16
MESH = pl.DeviceIdType.MESH

WAVE = 8.0
SOFT = 0.1
TWO_PI = 2.0 * math.pi
TURNS = WAVE / TWO_PI
TURNS2 = TURNS * TURNS
KAPPA = 1.0 / TWO_PI

C0 = 2.221441438377396
C1 = -0.9135295479465378
C2 = 0.11267874257383814
C3 = -0.006494477491585805

NY, NZ, NQ = 4, 8, 4
BLOCKS = NY * NZ
PACKETS = BLOCKS // 2
EARLY = 8
CHUNK = 16
LIST_AT = 14
LANES = 128
ROUND_AT = {3: 2, 4: 4, 5: 7, 6: 9}


def ring(d, n):
    return min(d, n - d)


OFFSETS = sorted(
    ((dy, dz) for dy in range(NY) for dz in range(NZ)),
    key=lambda o: (ring(o[0], NY) + ring(o[1], NZ), o),
)
HOPS = [ring(dy, NY) + ring(dz, NZ) for dy, dz in OFFSETS]
FARTHEST = max(HOPS)


def within(hops):
    return sum(h <= hops for h in HOPS)


def half_circle(turns):
    v = turns - jnp.round(turns)
    z = v * v
    s = v * (C0 + z * (C1 + z * (C2 + z * C3)))
    q = s * s
    w = 2.0 - q
    s2 = s * (w * lax.rsqrt(w))
    return 0.5 - s2 * s2, s2 * (1.0 - q)


def pair_kernel(turns2, facing):
    h = lax.rsqrt(turns2)
    cosine, sine = half_circle(turns2 * h)
    p = facing * (h * h)
    hk = h * KAPPA
    a = p * hk
    e = p + hk
    return a * cosine + e * sine, a * sine - e * cosine


def split3(x):
    hi = x.astype(BF16).astype(F32)
    rest = x - hi
    mid = rest.astype(BF16).astype(F32)
    return hi, mid, rest - mid


def split2(x):
    hi = x.astype(BF16)
    return hi, (x - hi.astype(F32)).astype(BF16)


def source_terms(geo):
    parts = split3(geo)
    count = geo.shape[1]
    row = lax.broadcasted_iota(jnp.int32, (4, count), 0)

    def stack(k):
        hi, mid, lo = (part[4 * k : 4 * k + 4] for part in parts)
        ones = jnp.where(row < 3, 1.0 if k == 0 else 0.0, 0.0)
        rows = [hi, mid, lo, hi, mid, hi, ones, jnp.zeros((4, count), F32)]
        return jnp.concatenate(rows, 0).T.astype(BF16)

    return jnp.concatenate([stack(0), stack(1)], 0)


def target_terms(pos):
    count = pos.shape[1]
    hi, mid, lo = split3(pos)
    square = split3(TURNS2 * jnp.sum(pos * pos, 0, keepdims=True))
    one = jnp.ones((1, count), F32)
    zero = jnp.zeros((1, count), F32)
    rows = [hi, one, hi, one, hi, one, mid, zero, mid, zero, lo, zero]
    rows += [square[0], square[1], square[2]] + [zero] * 5
    return jnp.concatenate(rows, 0).astype(BF16)


def kernel(
    pos_hbm, ang_hbm, area_hbm, den_hbm, owner_hbm, slot_hbm, index_hbm, coef_hbm, out_ref,
    pos_in, ang_in, area_in, den_in, owner_in, slot_in, index_in, coef_in,
    pkt, mine, other, tpos, lists, tf, terms, left, rf0, rf1, k0, k1, k2, k3, k4, k5, k6, k7, acc,
    listed, listed_got, part, part_got,
    in_sem, round_sem, swap_send, swap_recv, pkt_send, pkt_recv, den_send, den_recv,
    tpos_send, tpos_recv, lists_send, lists_recv, listed_send, listed_recv, part_send, part_recv,
):
    count = pos_hbm.shape[1]
    halves = count // LANES
    blk = lax.axis_index("blk")
    rhs = lax.axis_index("rhs")
    q = blk % NQ
    z = (blk // NQ) % NZ
    y = blk // (NQ * NZ)
    column_base = blk - q
    side = 1 - rhs
    zs = [lax.rem(z + d, NZ) * NQ + q for d in range(NZ)]
    ys = [lax.rem(y + d, NY) * (NZ * NQ) for d in range(NY)]
    qs = [lax.rem(q + d, NQ) for d in range(NQ)]

    def device(b, r):
        return {"blk": b, "rhs": r}

    def column(n):
        return qs[n // 2], (side if n % 2 else rhs)

    def plane(n):
        dy, dz = OFFSETS[n]
        return device(ys[(NY - dy) % NY] + zs[(NZ - dz) % NZ], rhs)

    barrier = pltpu.get_barrier_semaphore()
    near = within(1)
    for n in range(1, near):
        pl.semaphore_signal(barrier, inc=1, device_id=plane(n), device_id_type=MESH)
    for n in range(1, 2 * NQ):
        cq, cr = column(n)
        pl.semaphore_signal(
            barrier, inc=1, device_id=device(column_base + cq, cr), device_id_type=MESH
        )

    loads = [
        pltpu.make_async_copy(src, dst, in_sem.at[n])
        for n, (src, dst) in enumerate(
            [
                (pos_hbm, pos_in), (ang_hbm, ang_in), (area_hbm, area_in), (den_hbm, den_in),
                (owner_hbm, owner_in), (slot_hbm, slot_in), (index_hbm, index_in), (coef_hbm, coef_in),
            ]
        )
    ]
    for load in loads:
        load.start()
    for load in loads[:6]:
        load.wait()

    def own_half(v):
        return jnp.where(rhs == 0, v[:, 0:LANES], v[:, LANES : 2 * LANES])

    def other_half(v):
        return jnp.where(rhs == 0, v[:, LANES : 2 * LANES], v[:, 0:LANES])

    pos = pos_in[...]
    tpos[q] = pos
    lists[q] = jnp.concatenate([owner_in[...], slot_in[...]], 0)
    cosines, sines = half_circle(ang_in[...] * KAPPA)
    cosines = 2.0 * cosines
    sines = 2.0 * sines
    normal = jnp.concatenate(
        [cosines[0:1] * cosines[1:2], sines[0:1] * cosines[1:2], sines[1:2]], 0
    )
    weight = area_in[...] * (TURNS / math.sqrt(count * BLOCKS * NQ))
    density = den_in[0]
    sources = jnp.concatenate([density * weight, density], 0)
    mine[...] = other_half(sources)
    pkt[1, 0:8, 0:LANES] = own_half(
        jnp.concatenate(
            [
                (-2.0 * TURNS2) * pos,
                TURNS2 * (jnp.sum(pos * pos, 0, keepdims=True) + SOFT * SOFT),
                TURNS2 * normal,
                -TURNS2 * jnp.sum(pos * normal, 0, keepdims=True),
            ],
            0,
        )
    )

    pl.semaphore_wait(barrier, 2 * NQ - 1 + near - 1)

    swap = pltpu.make_async_remote_copy(
        src_ref=mine, dst_ref=other, send_sem=swap_send, recv_sem=swap_recv,
        device_id=device(blk, side), device_id_type=MESH,
    )

    def lanes_of(n):
        return pl.ds((n % 2) * LANES, LANES)

    def plane_copy(n, rows, send, recv):
        return pltpu.make_async_remote_copy(
            src_ref=pkt.at[1, rows, pl.ds(0, LANES)], dst_ref=pkt.at[n // 2 + 1, rows, lanes_of(n)],
            send_sem=send.at[n], recv_sem=recv.at[n],
            device_id=plane(n), device_id_type=MESH,
        )

    geo_rows, den_rows, all_rows = pl.ds(0, 8), pl.ds(8, 8), pl.ds(0, 16)

    def arrival(k, half, rows, recv):
        return pltpu.make_async_remote_copy(
            src_ref=pkt.at[1, rows, pl.ds(0, LANES)],
            dst_ref=pkt.at[k + 1, rows, pl.ds(half * LANES, LANES)],
            send_sem=swap_send, recv_sem=recv.at[2 * k + half],
            device_id=device(blk, side), device_id_type=MESH,
        )

    def sent(n, rows, send):
        return pltpu.make_async_remote_copy(
            src_ref=pkt.at[1, rows, pl.ds(0, LANES)], dst_ref=pkt.at[1, rows, pl.ds(0, LANES)],
            send_sem=send.at[n], recv_sem=swap_recv,
            device_id=device(blk, side), device_id_type=MESH,
        )

    def to_quarter(n, src, send, recv):
        return pltpu.make_async_remote_copy(
            src_ref=src.at[q], dst_ref=src.at[q], send_sem=send.at[n], recv_sem=recv.at[q],
            device_id=device(column_base + qs[n], rhs), device_id_type=MESH,
        )

    def from_quarter(n, src, send, recv):
        return pltpu.make_async_remote_copy(
            src_ref=src.at[q], dst_ref=src.at[qs[n]], send_sem=send.at[n], recv_sem=recv.at[qs[n]],
            device_id=device(column_base + qs[n], rhs), device_id_type=MESH,
        )

    def to_column(n, src, dst, send, recv):
        cq, cr = column(n)
        return pltpu.make_async_remote_copy(
            src_ref=src.at[2 * cq + cr], dst_ref=dst.at[2 * q + rhs],
            send_sem=send.at[n], recv_sem=recv.at[2 * q + rhs],
            device_id=device(column_base + cq, cr), device_id_type=MESH,
        )

    def from_column(n, src, dst, send, recv):
        cq, cr = column(n)
        return pltpu.make_async_remote_copy(
            src_ref=src.at[2 * cq + cr], dst_ref=dst.at[2 * cq + cr],
            send_sem=send.at[n], recv_sem=recv.at[2 * cq + cr],
            device_id=device(column_base + cq, cr), device_id_type=MESH,
        )

    def each(first, last, act):
        for n in range(first, last):
            act(n)

    def loop(first, last, act):
        def step(n, carry):
            act(n)
            return carry

        lax.fori_loop(first, last, step, 0)

    def tell(r):
        for n in range(1, near):
            pl.semaphore_signal(round_sem.at[r], inc=1, device_id=plane(n), device_id_type=MESH)

    def hear(r):
        pl.semaphore_wait(round_sem.at[r], near - 1)
        if r < FARTHEST:
            tell(r + 1)

    swap.start()
    tell(2)
    each(1, NQ, lambda n: to_quarter(n, tpos, tpos_send, tpos_recv).start())
    each(1, near, lambda n: plane_copy(n, geo_rows, pkt_send, pkt_recv).start())
    each(1, NQ, lambda n: to_quarter(n, lists, lists_send, lists_recv).start())

    def send_densities():
        swap.wait_recv()
        a = own_half(sources)
        b = other[...]
        first = jnp.where(rhs == 0, a, b)
        second = jnp.where(rhs == 0, b, a)
        pkt[1, 8:16, 0:LANES] = jnp.concatenate(
            [first[0:1], second[0:1], first[1:2], second[1:2], first[2:3], second[2:3], first[3:4], second[3:4]], 0
        )
        each(1, EARLY, lambda n: plane_copy(n, den_rows, den_send, den_recv).start())
        each(EARLY, within(2), lambda n: plane_copy(n, all_rows, pkt_send, pkt_recv).start())

    hear(2)
    each(near, EARLY, lambda n: plane_copy(n, geo_rows, pkt_send, pkt_recv).start())
    each(1, NQ, lambda n: from_quarter(n, tpos, tpos_send, tpos_recv).wait_recv())
    for j in range(NQ):
        tf[j] = target_terms(tpos[j])
    arrival(0, 1, geo_rows, pkt_recv).wait_recv()

    rf = (rf0, rf1)
    kk = (k0, k1, k2, k3, k4, k5, k6, k7)

    def products(j):
        for half in range(2):
            rows = slice(half * count, (half + 1) * count)
            rf[j % 2][rows] = jnp.dot(terms[rows], tf[j % NQ], preferred_element_type=F32)

    def pairs(j, b):
        for c in range(count // CHUNK):
            rows = slice(c * CHUNK, (c + 1) * CHUNK)
            real, imag = pair_kernel(
                rf[j % 2][rows], rf[j % 2][count + c * CHUNK : count + (c + 1) * CHUNK]
            )
            for n, piece in enumerate(split2(real) + split2(imag)):
                kk[b][n * count + c * CHUNK : n * count + (c + 1) * CHUNK] = piece

    def apply(j, b):
        acc[j] += jnp.dot(left[...], kk[b][...], preferred_element_type=F32)

    def density_terms(p):
        rows = pkt[p + 1, 8:12, :]
        turned = jnp.concatenate([-rows[2:4], rows[0:2]], 0)

        def both(v):
            hi = v.astype(BF16).astype(F32)
            return jnp.concatenate([hi, v - hi], 0).astype(BF16)

        real, imag = both(rows), both(turned)
        return jnp.concatenate([real, real, imag, imag], 1)

    terms[...] = source_terms(pkt[1, 0:8, :])
    products(0)
    send_densities()

    def look_up():
        each(1, NQ, lambda n: from_quarter(n, lists, lists_send, lists_recv).wait_recv())
        sub = lax.broadcasted_iota(jnp.int32, (8, LANES), 0)
        homes = []
        for group in range(PACKETS // 8):
            homes.append([])
            for t in range(halves):
                home = jnp.zeros((8, LANES), jnp.int32)
                for row in range(8):
                    dy, dz = OFFSETS[2 * (8 * group + row) + t]
                    home = jnp.where(sub == row, ys[dy] + zs[dz], home)
                homes[group].append(home)
        for j in range(NQ):
            for h in range(halves):
                cols = slice(h * LANES, (h + 1) * LANES)
                own = jnp.broadcast_to(lists[j, 0:1, cols], (8, LANES))
                place = jnp.broadcast_to(lists[j, 1:2, cols], (8, LANES))
                found = [jnp.zeros((8, LANES), F32) for _ in range(4)]
                for group in range(PACKETS // 8):
                    for t in range(halves):
                        hit = jnp.logical_and(own == homes[group][t], place // LANES == rhs)
                        for c in range(4):
                            table = pkt[8 * group + 1 : 8 * group + 9, 12 + c, t * LANES : (t + 1) * LANES]
                            value = jnp.take_along_axis(table, place % LANES, axis=1)
                            found[c] = found[c] + jnp.where(hit, value, 0.0)
                for c in range(4):
                    listed[2 * j + c % 2, c // 2 : c // 2 + 1, cols] = jnp.sum(found[c], 0, keepdims=True)
        each(1, 2 * NQ, lambda n: to_column(n, listed, listed_got, listed_send, listed_recv).start())

    def packet(p, now):
        then = 1 - now

        @pl.when(jnp.logical_and(p > 1, p <= EARLY // 2))
        def _():
            for half in range(2):
                arrival(p - 1, half, den_rows, den_recv).wait_recv()

        @pl.when(p == 1)
        def _():
            arrival(0, 1, den_rows, den_recv).wait_recv()
            acc[...] = jnp.zeros_like(acc)

        @pl.when(p + 1 < EARLY // 2)
        def _():
            for half in range(2):
                arrival(p + 1, half, geo_rows, pkt_recv).wait_recv()

        @pl.when(jnp.logical_and(p + 1 >= EARLY // 2, p < LIST_AT))
        def _():
            for half in range(2):
                arrival(p + 1, half, all_rows, pkt_recv).wait_recv()

        for r in range(3, FARTHEST + 1):
            if now == ROUND_AT[r] % 2:

                @pl.when(p == ROUND_AT[r])
                def _():
                    hear(r)
                    each(
                        within(r - 1),
                        within(r),
                        lambda n: plane_copy(n, all_rows, pkt_send, pkt_recv).start(),
                    )

        if now == LIST_AT % 2:

            @pl.when(p == LIST_AT)
            def _():
                for k in range(LIST_AT + 1, PACKETS):
                    for half in range(2):
                        arrival(k, half, all_rows, pkt_recv).wait_recv()
                look_up()

        left[...] = density_terms(p - 1)
        for j in range(NQ):
            if j == NQ - 1:
                terms[...] = source_terms(pkt[jnp.minimum(p + 2, PACKETS), 0:8, :])
            products(j + 1)
            apply(j, NQ * then + j)
            pairs(j, NQ * now + j)

    def body(i, carry):
        packet(2 * i, 0)
        packet(2 * i + 1, 1)
        return carry

    lax.fori_loop(0, PACKETS // 2, body, 0)
    left[...] = density_terms(PACKETS - 1)
    for j in range(NQ):
        apply(j, NQ + j)
    for j in range(NQ):
        total = acc[j]
        far = total[0:4] + total[4:8]
        for r in range(2):
            part[2 * j + r] = jnp.concatenate([far[r : r + 1], far[2 + r : 3 + r]], 0)
    each(1, 2 * NQ, lambda n: to_column(n, part, part_got, part_send, part_recv).start())

    loads[6].wait()
    loads[7].wait()
    me = 2 * q + rhs
    listed_got[me] = listed[me]
    each(1, 2 * NQ, lambda n: from_column(n, listed, listed_got, listed_send, listed_recv).wait_recv())
    mine_listed = jnp.sum(listed_got[...], 0)
    near = [[], []]
    neighbours = index_hbm.shape[0]
    tables = [
        [
            jnp.broadcast_to(mine_listed[c : c + 1, t * LANES : (t + 1) * LANES], (8, LANES))
            for t in range(halves)
        ]
        for c in range(2)
    ]
    for h in range(halves):
        cols = slice(h * LANES, (h + 1) * LANES)
        sums = [jnp.zeros((8, LANES), F32) for _ in range(2)]
        for m in range(neighbours // 8):
            rows = slice(8 * m, 8 * m + 8)
            where_to = index_in[rows, cols]
            looked = []
            for c in range(2):
                value = jnp.zeros((8, LANES), F32)
                for t in range(halves):
                    found = jnp.take_along_axis(tables[c][t], where_to % LANES, axis=1)
                    value = jnp.where(where_to // LANES == t, found, value)
                looked.append(value)
            real, imag = coef_in[0, rows, cols], coef_in[1, rows, cols]
            sums[0] = sums[0] + (real * looked[0] - imag * looked[1])
            sums[1] = sums[1] + (real * looked[1] + imag * looked[0])
        for c in range(2):
            near[c].append(jnp.sum(sums[c], 0, keepdims=True))
    near = jnp.concatenate([jnp.concatenate(row, 1) for row in near], 0)

    part_got[me] = part[me]

    swap.wait_send()
    loop(1, EARLY, lambda n: sent(n, geo_rows, pkt_send).wait_send())
    loop(1, EARLY, lambda n: sent(n, den_rows, den_send).wait_send())
    loop(EARLY, BLOCKS, lambda n: sent(n, all_rows, pkt_send).wait_send())
    each(1, NQ, lambda n: to_quarter(n, tpos, tpos_send, tpos_recv).wait_send())
    each(1, NQ, lambda n: to_quarter(n, lists, lists_send, lists_recv).wait_send())
    each(1, 2 * NQ, lambda n: to_column(n, listed, listed_got, listed_send, listed_recv).wait_send())
    each(1, 2 * NQ, lambda n: to_column(n, part, part_got, part_send, part_recv).wait_send())
    each(1, 2 * NQ, lambda n: from_column(n, part, part_got, part_send, part_recv).wait_recv())
    out_ref[0] = 0.5 * density + near + jnp.sum(part_got[...], 0)


def on_device(
    positions, normal_angles, areas, densities, need_owner, need_slot, near_index, near_coef
):
    count = positions.shape[1]
    args = (
        positions,
        normal_angles,
        areas.reshape(1, count),
        densities,
        need_owner.reshape(1, count),
        need_slot.reshape(1, count),
        near_index,
        near_coef,
    )
    dma = pltpu.SemaphoreType.DMA
    return pl.pallas_call(
        kernel,
        out_shape=jax.ShapeDtypeStruct((1, 2, count), F32),
        in_specs=[pl.BlockSpec(memory_space=pl.ANY)] * 8,
        out_specs=pl.BlockSpec(memory_space=pltpu.VMEM),
        scratch_shapes=[pltpu.VMEM(arg.shape, arg.dtype) for arg in args]
        + [
            pltpu.VMEM((PACKETS + 1, 16, count), F32),
            pltpu.VMEM((4, LANES), F32),
            pltpu.VMEM((4, LANES), F32),
            pltpu.VMEM((NQ, 3, count), F32),
            pltpu.VMEM((NQ, 2, count), jnp.int32),
            pltpu.VMEM((NQ, 32, count), BF16),
            pltpu.VMEM((2 * count, 32), BF16),
            pltpu.VMEM((8, 4 * count), BF16),
            pltpu.VMEM((2 * count, count), F32),
            pltpu.VMEM((2 * count, count), F32),
        ]
        + [pltpu.VMEM((4 * count, count), BF16)] * (2 * NQ)
        + [
            pltpu.VMEM((NQ, 8, count), F32),
            pltpu.VMEM((2 * NQ, 2, count), F32),
            pltpu.VMEM((2 * NQ, 2, count), F32),
            pltpu.VMEM((2 * NQ, 2, count), F32),
            pltpu.VMEM((2 * NQ, 2, count), F32),
            dma((8,)), pltpu.SemaphoreType.REGULAR((FARTHEST + 1,)), dma, dma,
            dma((BLOCKS,)), dma((BLOCKS,)), dma((EARLY,)), dma((EARLY,)),
            dma((NQ,)), dma((NQ,)), dma((NQ,)), dma((NQ,)),
            dma((2 * NQ,)), dma((2 * NQ,)), dma((2 * NQ,)), dma((2 * NQ,)),
        ],
        compiler_params=pltpu.CompilerParams(collective_id=0, has_side_effects=True),
        name="field",
    )(*args)


def solution(mesh):
    in_specs = (
        P(None, "blk"),
        P(None, "blk"),
        P("blk"),
        P("rhs", None, "blk"),
        P("blk", None),
        P("blk"),
        P(None, "blk"),
        P(None, None, "blk"),
    )
    return jax.shard_map(
        on_device, mesh=mesh, in_specs=in_specs, out_specs=P("rhs", None, "blk"), check_vma=False
    )
```

```python
import math

import jax
import jax.numpy as jnp
from jax import lax
from jax.experimental import pallas as pl
from jax.experimental.pallas import tpu as pltpu
from jax.sharding import PartitionSpec as P

F32 = jnp.float32
BF16 = jnp.bfloat16
MESH = pl.DeviceIdType.MESH

WAVE = 8.0
SOFT = 0.1
TWO_PI = 2.0 * math.pi
TURNS = WAVE / TWO_PI
TURNS2 = TURNS * TURNS
KAPPA = 1.0 / TWO_PI

C0 = 2.221441438377396
C1 = -0.9135295479465378
C2 = 0.11267874257383814
C3 = -0.006494477491585805

NY, NZ, NQ = 4, 8, 4
BLOCKS = NY * NZ
PACKETS = BLOCKS // 2
EARLY = 8
CHUNK = 16
LIST_AT = 14
LANES = 128
ROUND_AT = {3: 2, 4: 4, 5: 7, 6: 9}


def ring(d, n):
    return min(d, n - d)


OFFSETS = sorted(
    ((dy, dz) for dy in range(NY) for dz in range(NZ)),
    key=lambda o: (ring(o[0], NY) + ring(o[1], NZ), o),
)
HOPS = [ring(dy, NY) + ring(dz, NZ) for dy, dz in OFFSETS]
FARTHEST = max(HOPS)


def within(hops):
    return sum(h <= hops for h in HOPS)


def half_circle(turns):
    v = turns - jnp.round(turns)
    z = v * v
    s = v * (C0 + z * (C1 + z * (C2 + z * C3)))
    q = s * s
    w = 2.0 - q
    s2 = s * (w * lax.rsqrt(w))
    return 0.5 - s2 * s2, s2 * (1.0 - q)


def pair_kernel(turns2, facing):
    h = lax.rsqrt(turns2)
    cosine, sine = half_circle(turns2 * h)
    p = facing * (h * h)
    hk = h * KAPPA
    a = p * hk
    e = p + hk
    return a * cosine + e * sine, a * sine - e * cosine


def split3(x):
    hi = x.astype(BF16).astype(F32)
    rest = x - hi
    mid = rest.astype(BF16).astype(F32)
    return hi, mid, rest - mid


def split2(x):
    hi = x.astype(BF16)
    return hi, (x - hi.astype(F32)).astype(BF16)


def source_terms(geo):
    parts = split3(geo)
    count = geo.shape[1]
    row = lax.broadcasted_iota(jnp.int32, (4, count), 0)

    def stack(k):
        hi, mid, lo = (part[4 * k : 4 * k + 4] for part in parts)
        ones = jnp.where(row < 3, 1.0 if k == 0 else 0.0, 0.0)
        rows = [hi, mid, lo, hi, mid, hi, ones, jnp.zeros((4, count), F32)]
        return jnp.concatenate(rows, 0).T.astype(BF16)

    return jnp.concatenate([stack(0), stack(1)], 0)


def target_terms(pos):
    count = pos.shape[1]
    hi, mid, lo = split3(pos)
    square = split3(TURNS2 * jnp.sum(pos * pos, 0, keepdims=True))
    one = jnp.ones((1, count), F32)
    zero = jnp.zeros((1, count), F32)
    rows = [hi, one, hi, one, hi, one, mid, zero, mid, zero, lo, zero]
    rows += [square[0], square[1], square[2]] + [zero] * 5
    return jnp.concatenate(rows, 0).astype(BF16)


def kernel(
    pos_hbm, ang_hbm, area_hbm, den_hbm, owner_hbm, slot_hbm, index_hbm, coef_hbm, out_ref,
    pos_in, ang_in, area_in, den_in, owner_in, slot_in, index_in, coef_in,
    pkt, mine, other, tpos, lists, tf, terms, left, left_last, rf0, rf1, k0, k1, k2, k3, k4, k5, k6, k7, acc,
    listed, listed_got, part, part_got,
    in_sem, round_sem, swap_send, swap_recv, pkt_send, pkt_recv, den_send, den_recv,
    tpos_send, tpos_recv, lists_send, lists_recv, listed_send, listed_recv, part_send, part_recv,
):
    count = pos_hbm.shape[1]
    halves = count // LANES
    blk = lax.axis_index("blk")
    rhs = lax.axis_index("rhs")
    q = blk % NQ
    z = (blk // NQ) % NZ
    y = blk // (NQ * NZ)
    column_base = blk - q
    side = 1 - rhs
    zs = [lax.rem(z + d, NZ) * NQ + q for d in range(NZ)]
    ys = [lax.rem(y + d, NY) * (NZ * NQ) for d in range(NY)]
    qs = [lax.rem(q + d, NQ) for d in range(NQ)]

    def device(b, r):
        return {"blk": b, "rhs": r}

    def column(n):
        return qs[n // 2], (side if n % 2 else rhs)

    def plane(n):
        dy, dz = OFFSETS[n]
        return device(ys[(NY - dy) % NY] + zs[(NZ - dz) % NZ], rhs)

    barrier = pltpu.get_barrier_semaphore()
    near = within(1)
    for n in range(1, near):
        pl.semaphore_signal(barrier, inc=1, device_id=plane(n), device_id_type=MESH)
    for n in range(1, 2 * NQ):
        cq, cr = column(n)
        pl.semaphore_signal(
            barrier, inc=1, device_id=device(column_base + cq, cr), device_id_type=MESH
        )

    loads = [
        pltpu.make_async_copy(src, dst, in_sem.at[n])
        for n, (src, dst) in enumerate(
            [
                (pos_hbm, pos_in), (ang_hbm, ang_in), (area_hbm, area_in), (den_hbm, den_in),
                (owner_hbm, owner_in), (slot_hbm, slot_in), (index_hbm, index_in), (coef_hbm, coef_in),
            ]
        )
    ]
    for load in loads:
        load.start()
    for load in loads[:6]:
        load.wait()

    def own_half(v):
        return jnp.where(rhs == 0, v[:, 0:LANES], v[:, LANES : 2 * LANES])

    def other_half(v):
        return jnp.where(rhs == 0, v[:, LANES : 2 * LANES], v[:, 0:LANES])

    pos = pos_in[...]
    tpos[q] = pos
    lists[q] = jnp.concatenate([owner_in[...], slot_in[...]], 0)
    cosines, sines = half_circle(ang_in[...] * KAPPA)
    cosines = 2.0 * cosines
    sines = 2.0 * sines
    normal = jnp.concatenate(
        [cosines[0:1] * cosines[1:2], sines[0:1] * cosines[1:2], sines[1:2]], 0
    )
    weight = area_in[...] * (TURNS / math.sqrt(count * BLOCKS * NQ))
    density = den_in[0]
    sources = jnp.concatenate([density * weight, density], 0)
    mine[...] = other_half(sources)
    pkt[1, 0:8, 0:LANES] = own_half(
        jnp.concatenate(
            [
                (-2.0 * TURNS2) * pos,
                TURNS2 * (jnp.sum(pos * pos, 0, keepdims=True) + SOFT * SOFT),
                TURNS2 * normal,
                -TURNS2 * jnp.sum(pos * normal, 0, keepdims=True),
            ],
            0,
        )
    )

    pl.semaphore_wait(barrier, 2 * NQ - 1 + near - 1)

    swap = pltpu.make_async_remote_copy(
        src_ref=mine, dst_ref=other, send_sem=swap_send, recv_sem=swap_recv,
        device_id=device(blk, side), device_id_type=MESH,
    )

    def lanes_of(n):
        return pl.ds((n % 2) * LANES, LANES)

    def plane_copy(n, rows, send, recv):
        return pltpu.make_async_remote_copy(
            src_ref=pkt.at[1, rows, pl.ds(0, LANES)], dst_ref=pkt.at[n // 2 + 1, rows, lanes_of(n)],
            send_sem=send.at[n], recv_sem=recv.at[n],
            device_id=plane(n), device_id_type=MESH,
        )

    geo_rows, den_rows, all_rows = pl.ds(0, 8), pl.ds(8, 8), pl.ds(0, 16)

    def arrival(k, half, rows, recv):
        return pltpu.make_async_remote_copy(
            src_ref=pkt.at[1, rows, pl.ds(0, LANES)],
            dst_ref=pkt.at[k + 1, rows, pl.ds(half * LANES, LANES)],
            send_sem=swap_send, recv_sem=recv.at[2 * k + half],
            device_id=device(blk, side), device_id_type=MESH,
        )

    def sent(n, rows, send):
        return pltpu.make_async_remote_copy(
            src_ref=pkt.at[1, rows, pl.ds(0, LANES)], dst_ref=pkt.at[1, rows, pl.ds(0, LANES)],
            send_sem=send.at[n], recv_sem=swap_recv,
            device_id=device(blk, side), device_id_type=MESH,
        )

    def to_quarter(n, src, send, recv):
        return pltpu.make_async_remote_copy(
            src_ref=src.at[q], dst_ref=src.at[q], send_sem=send.at[n], recv_sem=recv.at[q],
            device_id=device(column_base + qs[n], rhs), device_id_type=MESH,
        )

    def from_quarter(n, src, send, recv):
        return pltpu.make_async_remote_copy(
            src_ref=src.at[q], dst_ref=src.at[qs[n]], send_sem=send.at[n], recv_sem=recv.at[qs[n]],
            device_id=device(column_base + qs[n], rhs), device_id_type=MESH,
        )

    def to_column(n, src, dst, send, recv):
        cq, cr = column(n)
        return pltpu.make_async_remote_copy(
            src_ref=src.at[2 * cq + cr], dst_ref=dst.at[2 * q + rhs],
            send_sem=send.at[n], recv_sem=recv.at[2 * q + rhs],
            device_id=device(column_base + cq, cr), device_id_type=MESH,
        )

    def from_column(n, src, dst, send, recv):
        cq, cr = column(n)
        return pltpu.make_async_remote_copy(
            src_ref=src.at[2 * cq + cr], dst_ref=dst.at[2 * cq + cr],
            send_sem=send.at[n], recv_sem=recv.at[2 * cq + cr],
            device_id=device(column_base + cq, cr), device_id_type=MESH,
        )

    def each(first, last, act):
        for n in range(first, last):
            act(n)

    def loop(first, last, act):
        def step(n, carry):
            act(n)
            return carry

        lax.fori_loop(first, last, step, 0)

    def tell(r):
        for n in range(1, near):
            pl.semaphore_signal(round_sem.at[r], inc=1, device_id=plane(n), device_id_type=MESH)

    def hear(r):
        pl.semaphore_wait(round_sem.at[r], near - 1)
        if r < FARTHEST:
            tell(r + 1)

    swap.start()
    tell(2)
    each(1, NQ, lambda n: to_quarter(n, tpos, tpos_send, tpos_recv).start())
    each(1, near, lambda n: plane_copy(n, geo_rows, pkt_send, pkt_recv).start())
    each(1, NQ, lambda n: to_quarter(n, lists, lists_send, lists_recv).start())

    def send_densities():
        swap.wait_recv()
        a = own_half(sources)
        b = other[...]
        first = jnp.where(rhs == 0, a, b)
        second = jnp.where(rhs == 0, b, a)
        pkt[1, 8:16, 0:LANES] = jnp.concatenate(
            [first[0:1], second[0:1], first[1:2], second[1:2], first[2:3], second[2:3], first[3:4], second[3:4]], 0
        )
        each(1, EARLY, lambda n: plane_copy(n, den_rows, den_send, den_recv).start())
        each(EARLY, within(2), lambda n: plane_copy(n, all_rows, pkt_send, pkt_recv).start())

    hear(2)
    each(near, EARLY, lambda n: plane_copy(n, geo_rows, pkt_send, pkt_recv).start())
    each(1, NQ, lambda n: from_quarter(n, tpos, tpos_send, tpos_recv).wait_recv())
    for j in range(NQ):
        tf[j] = target_terms(tpos[j])
    arrival(0, 1, geo_rows, pkt_recv).wait_recv()

    rf = (rf0, rf1)
    kk = (k0, k1, k2, k3, k4, k5, k6, k7)

    def products(j):
        for half in range(2):
            rows = slice(half * count, (half + 1) * count)
            rf[j % 2][rows] = jnp.dot(terms[rows], tf[j % NQ], preferred_element_type=F32)

    def pairs(j, b):
        for c in range(count // CHUNK):
            rows = slice(c * CHUNK, (c + 1) * CHUNK)
            real, imag = pair_kernel(
                rf[j % 2][rows], rf[j % 2][count + c * CHUNK : count + (c + 1) * CHUNK]
            )
            for n, piece in enumerate(split2(real) + split2(imag)):
                kk[b][n * count + c * CHUNK : n * count + (c + 1) * CHUNK] = piece

    def apply(j, b, lhs=left):
        acc[j] += jnp.dot(lhs[...], kk[b][...], preferred_element_type=F32)

    def density_terms(p):
        rows = pkt[p + 1, 8:12, :]
        turned = jnp.concatenate([-rows[2:4], rows[0:2]], 0)

        def both(v):
            hi = v.astype(BF16).astype(F32)
            return jnp.concatenate([hi, v - hi], 0).astype(BF16)

        real, imag = both(rows), both(turned)
        return jnp.concatenate([real, real, imag, imag], 1)

    terms[...] = source_terms(pkt[1, 0:8, :])
    products(0)
    send_densities()

    def look_up():
        each(1, NQ, lambda n: from_quarter(n, lists, lists_send, lists_recv).wait_recv())
        sub = lax.broadcasted_iota(jnp.int32, (8, LANES), 0)
        homes = []
        for group in range(PACKETS // 8):
            homes.append([])
            for t in range(halves):
                home = jnp.zeros((8, LANES), jnp.int32)
                for row in range(8):
                    dy, dz = OFFSETS[2 * (8 * group + row) + t]
                    home = jnp.where(sub == row, ys[dy] + zs[dz], home)
                homes[group].append(home)
        for j in range(NQ):
            for h in range(halves):
                cols = slice(h * LANES, (h + 1) * LANES)
                own = jnp.broadcast_to(lists[j, 0:1, cols], (8, LANES))
                place = jnp.broadcast_to(lists[j, 1:2, cols], (8, LANES))
                found = [jnp.zeros((8, LANES), F32) for _ in range(4)]
                for group in range(PACKETS // 8):
                    for t in range(halves):
                        hit = jnp.logical_and(own == homes[group][t], place // LANES == rhs)
                        for c in range(4):
                            table = pkt[8 * group + 1 : 8 * group + 9, 12 + c, t * LANES : (t + 1) * LANES]
                            value = jnp.take_along_axis(table, place % LANES, axis=1)
                            found[c] = found[c] + jnp.where(hit, value, 0.0)
                for c in range(4):
                    listed[2 * j + c % 2, c // 2 : c // 2 + 1, cols] = jnp.sum(found[c], 0, keepdims=True)
        each(1, 2 * NQ, lambda n: to_column(n, listed, listed_got, listed_send, listed_recv).start())

    def packet(p, now):
        then = 1 - now

        @pl.when(jnp.logical_and(p > 1, p <= EARLY // 2))
        def _():
            for half in range(2):
                arrival(p - 1, half, den_rows, den_recv).wait_recv()

        @pl.when(p == 1)
        def _():
            arrival(0, 1, den_rows, den_recv).wait_recv()
            acc[...] = jnp.zeros_like(acc)

        @pl.when(p + 1 < EARLY // 2)
        def _():
            for half in range(2):
                arrival(p + 1, half, geo_rows, pkt_recv).wait_recv()

        @pl.when(jnp.logical_and(p + 1 >= EARLY // 2, p < LIST_AT))
        def _():
            for half in range(2):
                arrival(p + 1, half, all_rows, pkt_recv).wait_recv()

        for r in range(3, FARTHEST + 1):
            if now == ROUND_AT[r] % 2:

                @pl.when(p == ROUND_AT[r])
                def _():
                    hear(r)
                    each(
                        within(r - 1),
                        within(r),
                        lambda n: plane_copy(n, all_rows, pkt_send, pkt_recv).start(),
                    )

        if now == LIST_AT % 2:

            @pl.when(p == LIST_AT)
            def _():
                for k in range(LIST_AT + 1, PACKETS):
                    for half in range(2):
                        arrival(k, half, all_rows, pkt_recv).wait_recv()
                look_up()

        left[...] = density_terms(p - 1)
        for j in range(NQ):
            if j == NQ - 1:
                terms[...] = source_terms(pkt[jnp.minimum(p + 2, PACKETS), 0:8, :])
            products(j + 1)
            apply(j, NQ * then + j)
            pairs(j, NQ * now + j)

    def body(i, carry):
        packet(2 * i, 0)
        packet(2 * i + 1, 1)
        return carry

    lax.fori_loop(0, PACKETS // 2 - 1, body, 0)
    packet(jnp.int32(PACKETS - 2), 0)
    left[...] = density_terms(PACKETS - 2)
    left_last[...] = density_terms(PACKETS - 1)
    for j in range(NQ):
        if j < NQ - 1:
            products(j + 1)
        apply(j, j)
        if j > 0:
            apply(j - 1, NQ + j - 1, left_last)
        pairs(j, NQ + j)
    apply(NQ - 1, 2 * NQ - 1, left_last)
    for j in range(NQ):
        total = acc[j]
        far = total[0:4] + total[4:8]
        for r in range(2):
            part[2 * j + r] = jnp.concatenate([far[r : r + 1], far[2 + r : 3 + r]], 0)
    each(1, 2 * NQ, lambda n: to_column(n, part, part_got, part_send, part_recv).start())

    loads[6].wait()
    loads[7].wait()
    me = 2 * q + rhs
    listed_got[me] = listed[me]
    each(1, 2 * NQ, lambda n: from_column(n, listed, listed_got, listed_send, listed_recv).wait_recv())
    mine_listed = jnp.sum(listed_got[...], 0)
    near = [[], []]
    neighbours = index_hbm.shape[0]
    tables = [
        [
            jnp.broadcast_to(mine_listed[c : c + 1, t * LANES : (t + 1) * LANES], (8, LANES))
            for t in range(halves)
        ]
        for c in range(2)
    ]
    for h in range(halves):
        cols = slice(h * LANES, (h + 1) * LANES)
        sums = [jnp.zeros((8, LANES), F32) for _ in range(2)]
        for m in range(neighbours // 8):
            rows = slice(8 * m, 8 * m + 8)
            where_to = index_in[rows, cols]
            looked = []
            for c in range(2):
                value = jnp.zeros((8, LANES), F32)
                for t in range(halves):
                    found = jnp.take_along_axis(tables[c][t], where_to % LANES, axis=1)
                    value = jnp.where(where_to // LANES == t, found, value)
                looked.append(value)
            real, imag = coef_in[0, rows, cols], coef_in[1, rows, cols]
            sums[0] = sums[0] + (real * looked[0] - imag * looked[1])
            sums[1] = sums[1] + (real * looked[1] + imag * looked[0])
        for c in range(2):
            near[c].append(jnp.sum(sums[c], 0, keepdims=True))
    near = jnp.concatenate([jnp.concatenate(row, 1) for row in near], 0)

    part_got[me] = part[me]

    swap.wait_send()
    loop(1, EARLY, lambda n: sent(n, geo_rows, pkt_send).wait_send())
    loop(1, EARLY, lambda n: sent(n, den_rows, den_send).wait_send())
    loop(EARLY, BLOCKS, lambda n: sent(n, all_rows, pkt_send).wait_send())
    each(1, NQ, lambda n: to_quarter(n, tpos, tpos_send, tpos_recv).wait_send())
    each(1, NQ, lambda n: to_quarter(n, lists, lists_send, lists_recv).wait_send())
    each(1, 2 * NQ, lambda n: to_column(n, listed, listed_got, listed_send, listed_recv).wait_send())
    each(1, 2 * NQ, lambda n: to_column(n, part, part_got, part_send, part_recv).wait_send())
    each(1, 2 * NQ, lambda n: from_column(n, part, part_got, part_send, part_recv).wait_recv())
    out_ref[0] = 0.5 * density + near + jnp.sum(part_got[...], 0)


def on_device(
    positions, normal_angles, areas, densities, need_owner, need_slot, near_index, near_coef
):
    count = positions.shape[1]
    args = (
        positions,
        normal_angles,
        areas.reshape(1, count),
        densities,
        need_owner.reshape(1, count),
        need_slot.reshape(1, count),
        near_index,
        near_coef,
    )
    dma = pltpu.SemaphoreType.DMA
    return pl.pallas_call(
        kernel,
        out_shape=jax.ShapeDtypeStruct((1, 2, count), F32),
        in_specs=[pl.BlockSpec(memory_space=pl.ANY)] * 8,
        out_specs=pl.BlockSpec(memory_space=pltpu.VMEM),
        scratch_shapes=[pltpu.VMEM(arg.shape, arg.dtype) for arg in args]
        + [
            pltpu.VMEM((PACKETS + 1, 16, count), F32),
            pltpu.VMEM((4, LANES), F32),
            pltpu.VMEM((4, LANES), F32),
            pltpu.VMEM((NQ, 3, count), F32),
            pltpu.VMEM((NQ, 2, count), jnp.int32),
            pltpu.VMEM((NQ, 32, count), BF16),
            pltpu.VMEM((2 * count, 32), BF16),
            pltpu.VMEM((8, 4 * count), BF16),
            pltpu.VMEM((8, 4 * count), BF16),
            pltpu.VMEM((2 * count, count), F32),
            pltpu.VMEM((2 * count, count), F32),
        ]
        + [pltpu.VMEM((4 * count, count), BF16)] * (2 * NQ)
        + [
            pltpu.VMEM((NQ, 8, count), F32),
            pltpu.VMEM((2 * NQ, 2, count), F32),
            pltpu.VMEM((2 * NQ, 2, count), F32),
            pltpu.VMEM((2 * NQ, 2, count), F32),
            pltpu.VMEM((2 * NQ, 2, count), F32),
            dma((8,)), pltpu.SemaphoreType.REGULAR((FARTHEST + 1,)), dma, dma,
            dma((BLOCKS,)), dma((BLOCKS,)), dma((EARLY,)), dma((EARLY,)),
            dma((NQ,)), dma((NQ,)), dma((NQ,)), dma((NQ,)),
            dma((2 * NQ,)), dma((2 * NQ,)), dma((2 * NQ,)), dma((2 * NQ,)),
        ],
        compiler_params=pltpu.CompilerParams(collective_id=0, has_side_effects=True),
        name="field",
    )(*args)


def solution(mesh):
    in_specs = (
        P(None, "blk"),
        P(None, "blk"),
        P("blk"),
        P("rhs", None, "blk"),
        P("blk", None),
        P("blk"),
        P(None, "blk"),
        P(None, None, "blk"),
    )
    return jax.shard_map(
        on_device, mesh=mesh, in_specs=in_specs, out_specs=P("rhs", None, "blk"), check_vma=False
    )
```
